512 devices in a mesh: ctx: 512 (over x, y, z, core).
Axes of the slice: x: 4, y: 4, z: 16, core: 2. Of those that a mesh axis runs over, the one named last changes fastest.
Arguments:
- query: bfloat16 [131072, 1280], P('ctx'), may hold values from -16 to 16
- key: bfloat16 [131072, 1280], P('ctx'), may hold values from -16 to 16
- value: bfloat16 [131072, 1280], P('ctx'), may hold values from -6 to 6
- grad_out: bfloat16 [131072, 1280], P('ctx'), may hold values from -16 to 16
- offsets: int32 [2, 10], replicated, may hold values from 0 to 255, as said below
Outputs:
- grad_query: bfloat16 [131072, 1280], P('ctx')
- grad_key: bfloat16 [131072, 1280], P('ctx')
- grad_value: bfloat16 [131072, 1280], P('ctx')
The draws below stay inside these ranges and needn't reach their ends.
Inputs may be any that keep to these rules, and one draw needn't show every extreme that they name: Row 0 holds 0 or 1 for each head, half of the heads taking each; row 1 holds distinct offsets below 256, one of them 256 - 1.
All inputs are finite; a program needn't handle non-finite values.
Results may differ from the reference program's by a relative error of at most 0.007.
Values may be sent and summed in bfloat16 or wider, within the bound.
A program may use at most 64 MiB of HBM per device.

```python
import math
import jax
import jax.numpy as jnp
from jax import lax

HEADS = 10
DH = 128
TOK_DEV = 256
TOPG = 128
TOKENS = 131072


def draw_query(key, part):
    extent = (TOKENS, HEADS * DH)
    return jnp.clip(jax.random.normal(jax.random.fold_in(key, 11), extent, jnp.float32), -6.0, 6.0).astype(jnp.bfloat16)


def draw_key(key, part):
    extent = (TOKENS, HEADS * DH)
    return jnp.clip(jax.random.normal(jax.random.fold_in(key, 12), extent, jnp.float32), -6.0, 6.0).astype(jnp.bfloat16)


def draw_offsets(key, part):
    pair_offsets = jax.random.permutation(jax.random.fold_in(key, 41), HEADS).astype(jnp.int32) % 2
    far_offsets = jax.random.permutation(jax.random.fold_in(key, 42), TOK_DEV - 1)[:HEADS - 1].astype(jnp.int32)
    far_offsets = jnp.concatenate([far_offsets, jnp.full((1,), TOK_DEV - 1, jnp.int32)])
    far_offsets = jax.random.permutation(jax.random.fold_in(key, 43), far_offsets)
    return jnp.stack([pair_offsets, far_offsets]).astype(jnp.int32)


def level_of(key, shape, cuts, least, top_value):
    gain, own = 1.0, jax.random.fold_in(key, 6)
    for dim, parts in cuts:
        steps = jnp.exp(jax.random.uniform(jax.random.fold_in(own, dim), (parts,), jnp.float32, least / len(cuts), top_value / len(cuts)))
        gain = gain * jnp.repeat(steps, shape[dim] // parts).reshape([-1 if axis == dim else 1 for axis in range(len(shape))])
    return gain


def normal_values(own_key, shape, deviation, limit, shards=(), held_as=jnp.bfloat16):
    level = level_of(own_key, shape, shards, -0.22, 0.18) if shards else 1.0
    drawn = jax.random.normal(own_key, shape, jnp.float32) * deviation * level
    return jnp.minimum(jnp.maximum(drawn, -limit), limit).astype(held_as)


def setup_inputs(seed: int = 0) -> dict:
    arg_keys = jax.random.split(jax.random.key(seed), 6)
    return {
        "query": draw_query(jax.random.fold_in(arg_keys[5], 71), 0),
        "key": draw_key(jax.random.fold_in(arg_keys[5], 71), 0),
        "value": normal_values(arg_keys[2], (TOKENS, HEADS * DH), 1.0, 6.0, ((0, 512),)),
        "grad_out": normal_values(arg_keys[3], (TOKENS, HEADS * DH), 4.0, 16.0, ((0, 512),)),
        "offsets": draw_offsets(jax.random.fold_in(arg_keys[5], 71), 0),
    }


def onehot_table(dilation, offset_row, dtype):
    return (jnp.arange(dilation, dtype=jnp.int32)[:, None] == offset_row[None, :].astype(jnp.int32)).astype(dtype)


def level_select(source, segment_width, dilation, offset_row):
    length, head_count, head_size = source.shape
    selector = onehot_table(dilation, offset_row, source.dtype)
    grouped = source.reshape(length // segment_width, segment_width // dilation, dilation, head_count, head_size)
    return jnp.sum(grouped * selector[None, None, :, :, None], axis=2)


def level_place(source, dilation, offset_row):
    segments, members, head_count, head_size = source.shape
    selector = onehot_table(dilation, offset_row, source.dtype)
    spread = source[:, :, None] * selector[None, None, :, :, None]
    return spread.reshape(segments * members * dilation, head_count, head_size)


def stat_select(source, segment_width, dilation, offset_row):
    head_count, length = source.shape
    selector = onehot_table(dilation, offset_row, source.dtype)
    grouped = source.reshape(head_count, length // segment_width, segment_width // dilation, dilation)
    return jnp.transpose(jnp.sum(grouped * selector.T[:, None, None, :], axis=3), (1, 0, 2))


def stat_place(source, dilation, offset_row):
    segments, head_count, members = source.shape
    selector = onehot_table(dilation, offset_row, source.dtype)
    spread = jnp.transpose(source, (1, 0, 2))[:, :, :, None] * selector.T[:, None, None, :]
    return spread.reshape(head_count, segments * members * dilation)


def segment_map(kernel, operands):
    segments = operands[0].shape[0]
    per_batch = math.gcd(segments, 8)
    batched = tuple(operand.reshape((segments // per_batch, per_batch) + operand.shape[1:]) for operand in operands)
    results = lax.map(lambda member: kernel(*member), batched)
    return tuple(result.reshape((segments,) + result.shape[2:]) for result in results)


def forward_block(queries, keys_in, values_in):
    factor = queries.shape[-1] ** -0.5
    scores = jnp.einsum("gmhc,gnhc->ghmn", queries.astype(jnp.float32), keys_in.astype(jnp.float32)) * factor
    row_peak = jnp.max(scores, axis=-1)
    powered = jnp.exp(scores - row_peak[..., None])
    row_total = jnp.sum(powered, axis=-1)
    rounded = lax.optimization_barrier(powered.astype(jnp.bfloat16)).astype(jnp.float32)
    blended = jnp.einsum("ghmn,gnhc->gmhc", rounded, values_in.astype(jnp.float32))
    return row_peak, row_total, blended


def backward_block(queries, keys_in, values_in, out_grads, log_total, row_delta):
    factor = queries.shape[-1] ** -0.5
    queries_wide = queries.astype(jnp.float32)
    keys_wide = keys_in.astype(jnp.float32)
    values_wide = values_in.astype(jnp.float32)
    grads_wide = out_grads.astype(jnp.float32)
    scores = jnp.einsum("gmhc,gnhc->ghmn", queries_wide, keys_wide) * factor
    chances = jnp.exp(scores - log_total[..., None])
    rounded = lax.optimization_barrier(chances.astype(jnp.bfloat16)).astype(jnp.float32)
    value_grad = jnp.einsum("ghmn,gmhc->gnhc", rounded, grads_wide)
    product_grad = jnp.einsum("gmhc,gnhc->ghmn", grads_wide, values_wide)
    score_grad = (factor * chances * (product_grad - row_delta[..., None])).astype(jnp.bfloat16)
    score_grad = lax.optimization_barrier(score_grad).astype(jnp.float32)
    query_grad = jnp.einsum("ghmn,gnhc->gmhc", score_grad, keys_wide)
    key_grad = jnp.einsum("ghmn,gmhc->gnhc", score_grad, queries_wide)
    return query_grad, key_grad, value_grad


def reference(query, key, value, grad_out, offsets):
    head_count = offsets.shape[1]
    length = query.shape[0]
    head_size = query.shape[1] // head_count
    operands = [operand.reshape(length, head_count, head_size) for operand in (query, key, value, grad_out)]
    plan = ((TOK_DEV, 1, jnp.zeros((head_count,), jnp.int32)), (2 * TOK_DEV, 2, offsets[0]), (TOPG * TOK_DEV, TOK_DEV, offsets[1]))
    picked = []
    peaks = []
    totals = []
    blends = []
    masks = []
    for segment_width, dilation, offset_row in plan:
        selected = [level_select(operand, segment_width, dilation, offset_row) for operand in operands]
        level_peak, level_total, level_blend = segment_map(forward_block, tuple(selected[:3]))
        picked.append(selected)
        peaks.append(stat_place(level_peak, dilation, offset_row))
        totals.append(stat_place(level_total, dilation, offset_row))
        blends.append(level_place(level_blend, dilation, offset_row))
        masks.append(stat_place(jnp.ones_like(level_peak), dilation, offset_row))
    row_peak = peaks[0]
    for level in (1, 2):
        row_peak = jnp.maximum(row_peak, jnp.where(masks[level] > 0, peaks[level], peaks[0]))
    weights = [jnp.exp(peaks[0] - row_peak)]
    for level in (1, 2):
        weights.append(masks[level] * jnp.exp(jnp.where(masks[level] > 0, peaks[level], row_peak) - row_peak))
    row_total = totals[0] * weights[0] + totals[1] * weights[1] + totals[2] * weights[2]
    blended = blends[0] * weights[0].T[:, :, None] + blends[1] * weights[1].T[:, :, None] + blends[2] * weights[2].T[:, :, None]
    attended = blended / row_total.T[:, :, None]
    log_total = row_peak + jnp.log(row_total)
    row_delta = jnp.sum(operands[3].astype(jnp.float32) * attended, axis=-1).T
    gradients = []
    for (segment_width, dilation, offset_row), selected in zip(plan, picked):
        level_log = stat_select(log_total, segment_width, dilation, offset_row)
        level_delta = stat_select(row_delta, segment_width, dilation, offset_row)
        results = segment_map(backward_block, (selected[0], selected[1], selected[2], selected[3], level_log, level_delta))
        gradients.append([level_place(result, dilation, offset_row) for result in results])
    finals = []
    for which in range(3):
        summed = gradients[0][which] + gradients[1][which] + gradients[2][which]
        finals.append(summed.astype(jnp.bfloat16).reshape(length, head_count * head_size))
    return (finals[0], finals[1], finals[2])
```

```python
import jax
import jax.numpy as jnp
from jax import lax
from jax.experimental import pallas as pl
from jax.experimental.pallas import tpu as pltpu
from jax.sharding import PartitionSpec as P

MESH = pl.DeviceIdType.MESH
HEADS = 10
DH = 128
TOK = 256
HALF = TOK // 2
WIDTH = HEADS * DH
GROUP = 16
ZGROUPS = 8
FACTOR = DH**-0.5
SCALE2 = FACTOR * 1.4426950408889634
LOW = -1e30
F32 = jnp.float32
BF16 = jnp.bfloat16

NN = (((1,), (0,)), ((), ()))
NT = (((1,), (1,)), ((), ()))
TN = (((0,), (0,)), ((), ()))


def mm(a, b, dims):
    return lax.dot_general(a, b, dims, preferred_element_type=F32)


def iota(shape, dim):
    return lax.broadcasted_iota(jnp.int32, shape, dim)


def split(x):
    high = x.astype(BF16)
    return high, (x - high.astype(F32)).astype(BF16)


def kernel(
    off, q_hbm, k_hbm, v_hbm, g_hbm, oq, ok, ov,
    x, px, pr, qr, sb, pb, sc, pc, tt, ts, rs, rb, lx, lr, acc, ls, ws, wx, w2, qp, wd,
    ld_sem, px_send, px_recv, p1_send, p1_recv, c1_send, c1_recv,
    p2_send, p2_recv, c2_send, c2_recv, p3_send, p3_recv, lx_send, lx_recv,
):
    me = lax.axis_index("ctx")
    core = lax.rem(me, 2)
    z = lax.rem(lax.div(me, 2), 16)
    y = lax.rem(lax.div(me, 32), 4)
    base = lax.div(me, 128) * 128
    zg = lax.div(z, 2)
    zl = lax.rem(z, 2)
    low = zl * 2 + core
    m = y * 4 + low
    mine = (lax.rem(low, 2) * 2 + lax.div(low, 2)) * 4 + y
    owner = mine < HEADS

    def member(j):
        return (base + lax.div(j, 4) * 32 + (zg * 2 + lax.rem(lax.div(j, 2), 2)) * 2 + lax.rem(j, 2),)

    def zpeer(g):
        return (base + y * 32 + (g * 2 + zl) * 2 + core,)

    def owner_of(h):
        k = lax.div(h, 4)
        return lax.rem(h, 4) * 4 + lax.rem(k, 2) * 2 + lax.div(k, 2)

    partner = (me + 1 - 2 * core,)

    def remote(src, dst, send, recv, device):
        return pltpu.make_async_remote_copy(
            src_ref=src, dst_ref=dst, send_sem=send, recv_sem=recv, device_id=device, device_id_type=MESH
        )

    loads = [
        pltpu.make_async_copy(ref, x.at[i], ld_sem.at[i]) for i, ref in enumerate((q_hbm, k_hbm, v_hbm, g_hbm))
    ]
    for load in loads:
        load.start()

    barrier = pltpu.get_barrier_semaphore()

    @pl.loop(1, GROUP)
    def _(d):
        pl.semaphore_signal(barrier, inc=1, device_id=member(lax.rem(m + d, GROUP)), device_id_type=MESH)

    @pl.loop(1, ZGROUPS)
    def _(d):
        pl.semaphore_signal(barrier, inc=1, device_id=zpeer(lax.rem(zg + d, ZGROUPS)), device_id_type=MESH)

    lane_head = lax.div(iota((8, WIDTH), 1), DH)
    off_lane = jnp.zeros((8, WIDTH), jnp.int32)
    row16 = iota((16, TOK), 0)
    off0 = jnp.zeros((16, TOK), jnp.int32)
    off1 = jnp.zeros((16, TOK), jnp.int32)
    for h in range(HEADS):
        off_lane = jnp.where(lane_head == h, off[0, h], off_lane)
        off0 = jnp.where(row16 == h, off[0, h], off0)
        off1 = jnp.where(row16 == h, off[1, h], off1)
    lane16 = iota((16, TOK), 1)
    sel_wide = (lane16 == off1).astype(F32).astype(BF16)
    row_in_pair = lax.rem(off1, 2) == off0
    key_in_pair = lax.rem(lane16, 2) == off0
    both = jnp.logical_and(row_in_pair, key_in_pair)
    weight_wide = jnp.where(both, 2.0, 1.0)
    block = lax.div(iota((16, WIDTH), 1), DH) == iota((16, WIDTH), 0)
    perm_row = iota((TOK, TOK), 0)
    perm_to = jnp.where(perm_row < HALF, 2 * perm_row, 2 * perm_row - (TOK - 1))
    perm = (iota((TOK, TOK), 1) == perm_to).astype(F32).astype(BF16)
    off_wide = off_lane[0:1, :] > 0

    sb[...] = jnp.zeros_like(sb)
    sc[...] = jnp.zeros_like(sc)
    rb[...] = jnp.zeros_like(rb)
    rs[...] = jnp.zeros_like(rs)
    ls[...] = jnp.zeros_like(ls)

    for i in range(4):
        loads[i].wait()
        picked = jnp.where(block, mm(sel_wide, x[i], NN), 0.0)
        qr[i] = picked.astype(BF16)
        for h in range(HEADS):
            sb[8 * h + i : 8 * h + i + 1, :] = picked[h : h + 1, h * DH : (h + 1) * DH]
    for i in range(4):
        parts = mm(perm, x[i], NN)
        px[i] = jnp.where(off_wide, parts[HALF:], parts[:HALF]).astype(BF16)

    pl.semaphore_wait(barrier, GROUP + ZGROUPS - 2)

    def rows_of(j):
        return pl.ds(pl.multiple_of(8 * j, 8), 8)

    def to_owner(src, dst, send, recv, h):
        return remote(src.at[rows_of(h)], dst.at[rows_of(m)], send.at[h], recv, member(owner_of(h)))

    def send_to_owners(src, dst, send, recv):
        @pl.loop(0, HEADS)
        def _(h):
            @pl.when(owner_of(h) != m)
            def _():
                to_owner(src, dst, send, recv, h).start()

            @pl.when(owner_of(h) == m)
            def _():
                pltpu.make_async_copy(src.at[rows_of(h)], dst.at[rows_of(m)], recv).start()

    def wait_sent(src, dst, send, recv):
        @pl.loop(0, HEADS)
        def _(h):
            @pl.when(owner_of(h) != m)
            def _():
                to_owner(src, dst, send, recv, h).wait_send()

    pair_copies = [remote(px.at[i], pr.at[i], px_send.at[i], px_recv.at[i], partner) for i in range(4)]
    pair_copies[1].start()
    pair_copies[2].start()
    send_to_owners(sb, pb, p1_send, p1_recv)
    pair_copies[0].start()
    pair_copies[3].start()

    s_own = mm(qr[0], x[1], NT) * SCALE2
    x_own = mm(qr[3], x[2], NT)
    pair_copies[1].wait_recv()
    pair_copies[2].wait_recv()
    s_cross = jnp.where(row_in_pair[:, :HALF], mm(qr[0], pr[1], NT) * SCALE2, LOW)
    x_cross = mm(qr[3], pr[2], NT)
    peak = jnp.maximum(jnp.max(s_own, 1, keepdims=True), jnp.max(s_cross, 1, keepdims=True))
    e_own = jnp.exp2(s_own - peak) * weight_wide
    e_cross = jnp.exp2(s_cross - peak)
    total = jnp.sum(e_own, 1, keepdims=True) + jnp.sum(e_cross, 1, keepdims=True)
    blend = jnp.sum(e_own * x_own, 1, keepdims=True) + jnp.sum(e_cross * x_cross, 1, keepdims=True)
    lane128 = iota((16, DH), 1)
    wide_stats = jnp.where(lane128 == 0, peak + jnp.log2(total), jnp.where(lane128 == 1, blend / total, 0.0))
    for h in range(HEADS):
        sc[8 * h : 8 * h + 1, :] = wide_stats[h : h + 1, :]
    send_to_owners(sc, pc, c1_send, c1_recv)
    ws[0] = s_own
    ws[1] = x_own
    wx[0] = s_cross
    wx[1] = x_cross

    def to_zpeer(src, send, recv, d):
        return remote(src.at[zg], src.at[zg], send.at[d], recv, zpeer(lax.rem(zg + d, ZGROUPS)))

    @pl.when(owner)
    def _():
        pltpu.make_async_copy(pb, pb, p1_recv).wait()
        for i in range(4):
            tt[zg, i] = pb[pl.ds(i, GROUP, stride=8), :].astype(BF16)

        @pl.loop(1, ZGROUPS)
        def _(d):
            to_zpeer(tt, p2_send, p2_recv, d).start()

    @pl.when(owner)
    def _():
        pltpu.make_async_copy(pc, pc, c1_recv).wait()
        ts[zg] = pc[pl.ds(0, GROUP, stride=8), :]

        @pl.loop(1, ZGROUPS)
        def _(d):
            to_zpeer(ts, c2_send, c2_recv, d).start()

    pair_copies[0].wait_recv()
    pair_copies[3].wait_recv()
    lane_pair = iota((16, HALF), 1)
    sel_pair = jnp.logical_and(row_in_pair[:, :HALF], lane_pair == lax.div(off1[:, :HALF], 2))
    sel_pair = sel_pair.astype(F32).astype(BF16)
    qp[0] = jnp.where(block, mm(sel_pair, pr[0], NN), 0.0).astype(BF16)
    qp[1] = jnp.where(block, mm(sel_pair, pr[3], NN), 0.0).astype(BF16)
    w2[0] = jnp.where(both, mm(qp[0], x[1], NT) * SCALE2, LOW)
    w2[1] = mm(qp[1], x[2], NT)

    lane_row = iota((1, TOK), 1)
    parity_lane = lax.rem(lane_row, 2)
    parity_row = lax.rem(iota((TOK, HALF), 0), 2)
    parity_row2 = lax.rem(iota((TOK, TOK), 0), 2)

    @pl.loop(0, HEADS)
    def _(h):
        hs = pl.ds(pl.multiple_of(h * DH, DH), DH)
        qh = x[0, :, hs]
        gh = x[3, :, hs]
        kh = x[1, :, hs]
        vh = x[2, :, hs]
        kx = pr[1, :, hs]
        vx = pr[2, :, hs]
        chosen = parity_lane == off[0, h]
        keep = jnp.where(lane_row == off[1, h], 0.0, 1.0)
        weight = jnp.where(jnp.logical_and(parity_row2 == off[0, h], chosen), 2.0, 1.0)
        s0 = mm(kh, qh, NT) * SCALE2
        s1 = mm(kx, qh, NT) * SCALE2 + jnp.where(chosen, 0.0, LOW)
        x0 = mm(vh, gh, NT)
        x1 = mm(vx, gh, NT)
        top = jnp.maximum(jnp.max(s0, 0, keepdims=True), jnp.max(s1, 0, keepdims=True))
        e0 = jnp.exp2(s0 - top) * weight
        e1 = jnp.exp2(s1 - top)
        tot = jnp.sum(e0, 0, keepdims=True) + jnp.sum(e1, 0, keepdims=True)
        num = jnp.sum(e0 * x0, 0, keepdims=True) + jnp.sum(e1 * x1, 0, keepdims=True)
        inv = 1.0 / tot
        delta = num * inv
        ls[0, pl.ds(h, 1), :] = jnp.where(keep > 0, top + jnp.log2(tot), -LOW)
        ls[1, pl.ds(h, 1), :] = delta
        gain = inv * keep
        p0 = e0 * gain
        p1 = e1 * gain
        d0 = ((p0 * FACTOR) * (x0 - delta)).astype(BF16)
        d1 = ((p1 * FACTOR) * (x1 - delta)).astype(BF16)
        acc[2, :, hs] = mm(p0.astype(BF16), gh, NN)
        acc[1, :, hs] = mm(d0, qh, NN)
        acc[0, :, hs] = mm(d0, kh, TN) + mm(d1, kx, TN)

    perm_t = jnp.where(iota((TOK, TOK), 1) < HALF, 2 * iota((TOK, TOK), 1), 2 * iota((TOK, TOK), 1) - (TOK - 1))
    perm_t = (iota((TOK, TOK), 0) == perm_t).astype(F32).astype(BF16)
    for i in range(2):
        value = ls[i]
        high, rest = split(value)
        mid, least = split(value - high.astype(F32))
        moved = mm(high, perm_t, NN) + (mm(mid, perm_t, NN) + mm(least, perm_t, NN))
        lx[i] = jnp.where(off0[:, :HALF] > 0, moved[:, HALF:], moved[:, :HALF])
    stat_copy = remote(lx, lr, lx_send, lx_recv, partner)
    stat_copy.start()
    stat_copy.wait_recv()

    @pl.loop(0, HEADS)
    def _(h):
        hs = pl.ds(pl.multiple_of(h * DH, DH), DH)
        kh = x[1, :, hs]
        vh = x[2, :, hs]
        qx = pr[0, :, hs]
        gx = pr[3, :, hs]
        lse = lr[0, pl.ds(h, 1), :]
        delta = lr[1, pl.ds(h, 1), :]
        s2 = mm(kh, qx, NT) * SCALE2
        x2 = mm(vh, gx, NT)
        p2 = jnp.exp2(jnp.where(parity_row == off[0, h], s2 - lse, LOW))
        d2 = ((p2 * FACTOR) * (x2 - delta)).astype(BF16)
        acc[2, :, hs] += mm(p2.astype(BF16), gx, NN)
        acc[1, :, hs] += mm(d2, qx, NN)

    def to_member(d):
        j = lax.rem(m + d, GROUP)
        return remote(rs.at[rows_of(j)], rb.at[rows_of(mine)], p3_send.at[d], p3_recv, member(j))

    @pl.when(owner)
    def _():
        seven = pl.ds(0, ZGROUPS - 1)
        pltpu.make_async_copy(tt.at[seven], tt.at[seven], p2_recv).wait()
        pltpu.make_async_copy(ts.at[seven], ts.at[seven], c2_recv).wait()
        qw, kw, vw, gw = [tt[:, i].reshape(128, DH) for i in range(4)]
        stat = ts[...].reshape(128, DH)
        lse_lp, delta_lp = stat[:, 0:1], stat[:, 1:2]
        s = mm(qw, kw, NT) * SCALE2
        xx = mm(gw, vw, NT)
        top = jnp.max(s, 1, keepdims=True)
        e = jnp.exp2(s - top)
        tot = jnp.sum(e, 1, keepdims=True)
        num = jnp.sum(e * xx, 1, keepdims=True)
        peak = jnp.maximum(top, lse_lp)
        c_w = jnp.exp2(top - peak)
        c_lp = jnp.exp2(lse_lp - peak)
        all_tot = tot * c_w + c_lp
        lse = peak + jnp.log2(all_tot)
        delta = (num * c_w + delta_lp * c_lp) / all_tot
        p = e * (c_w / all_tot)
        ds = ((p * FACTOR) * (xx - delta)).astype(BF16)
        wd[0] = mm(ds, kw, NN)
        wd[1] = mm(ds, qw, TN)
        wd[2] = mm(p.astype(BF16), gw, TN)
        lane = iota((128, DH), 1)
        both_stats = jnp.where(lane == 0, lse, jnp.where(lane == 1, delta, 0.0))
        wd[3] = both_stats
        own = pl.ds(pl.multiple_of(zg * GROUP, GROUP), GROUP)
        for i in range(4):
            rs[pl.ds(i, GROUP, stride=8), :] = wd[i, own, :]
        stats16 = wd[3, own, :]
        even = lax.rem(iota((GROUP, DH), 0), 2) == 0
        swapped = jnp.where(even, pltpu.roll(stats16, GROUP - 1, 0), pltpu.roll(stats16, 1, 0))
        rs[pl.ds(4, GROUP, stride=8), :] = swapped

        @pl.loop(1, GROUP)
        def _(d):
            to_member(d).start()

        pltpu.make_async_copy(rs.at[rows_of(m)], rb.at[rows_of(mine)], p3_recv).start()

    got = pl.ds(0, 8 * HEADS)
    pltpu.make_async_copy(rb.at[got], rb.at[got], p3_recv).wait()

    own_stat = rb[pl.ds(3, 16, stride=8), :]
    far_stat = rb[pl.ds(4, 16, stride=8), :]
    lse_r, delta_r = own_stat[:, 0:1], own_stat[:, 1:2]
    lse_f, delta_f = far_stat[:, 0:1], far_stat[:, 1:2]
    p_own = jnp.exp2(ws[0] - lse_r) * weight_wide
    d_own = ((p_own * FACTOR) * (ws[1] - delta_r)).astype(BF16)
    p_cross = jnp.exp2(wx[0] - lse_r)
    d_cross = ((p_cross * FACTOR) * (wx[1] - delta_r)).astype(BF16)
    p_far = jnp.exp2(w2[0] - lse_f)
    d_far = ((p_far * FACTOR) * (w2[1] - delta_f)).astype(BF16)

    def spread(i):
        row = rb[pl.ds(i, 16, stride=8), :]
        return jnp.where(block, jnp.concatenate([row] * HEADS, axis=1), 0.0)

    dq_row = jnp.where(block, mm(d_own, x[1], NN) + mm(d_cross, pr[1], NN), 0.0) + spread(0)
    sel = sel_wide
    fixes = (
        (oq, 0, jnp.concatenate([sel, sel], 0), jnp.concatenate(split(dq_row), 0)),
        (ok, 1, jnp.concatenate([d_own, d_far, sel, sel], 0), jnp.concatenate([qr[0], qp[0], *split(spread(1))], 0)),
        (
            ov,
            2,
            jnp.concatenate([p_own.astype(BF16), p_far.astype(BF16), sel, sel], 0),
            jnp.concatenate([qr[3], qp[1], *split(spread(2))], 0),
        ),
    )
    for ref, i, left, right in fixes:
        ref[...] = (acc[i] + mm(left, right, TN)).astype(BF16)

    for copy in pair_copies:
        copy.wait_send()
    stat_copy.wait_send()
    wait_sent(sb, pb, p1_send, p1_recv)
    wait_sent(sc, pc, c1_send, c1_recv)

    @pl.when(owner)
    def _():
        @pl.loop(1, ZGROUPS)
        def _(d):
            to_zpeer(tt, p2_send, p2_recv, d).wait_send()
            to_zpeer(ts, c2_send, c2_recv, d).wait_send()

        @pl.loop(1, GROUP)
        def _(d):
            to_member(d).wait_send()


def on_device(query, key, value, grad_out, offsets):
    shape = jax.ShapeDtypeStruct((TOK, WIDTH), BF16)
    vmem = pltpu.VMEM
    dma = pltpu.SemaphoreType.DMA
    return pl.pallas_call(
        kernel,
        out_shape=(shape, shape, shape),
        in_specs=[pl.BlockSpec(memory_space=pltpu.SMEM)] + [pl.BlockSpec(memory_space=pl.ANY)] * 4,
        out_specs=(pl.BlockSpec(memory_space=vmem),) * 3,
        scratch_shapes=[
            vmem((4, TOK, WIDTH), BF16),
            vmem((4, HALF, WIDTH), BF16),
            vmem((4, HALF, WIDTH), BF16),
            vmem((4, 16, WIDTH), BF16),
            vmem((8 * HEADS, DH), F32),
            vmem((8 * GROUP, DH), F32),
            vmem((8 * HEADS, DH), F32),
            vmem((8 * GROUP, DH), F32),
            vmem((ZGROUPS, 4, GROUP, DH), BF16),
            vmem((ZGROUPS, GROUP, DH), F32),
            vmem((8 * GROUP, DH), F32),
            vmem((8 * 16, DH), F32),
            vmem((2, 16, HALF), F32),
            vmem((2, 16, HALF), F32),
            vmem((3, TOK, WIDTH), F32),
            vmem((2, 16, TOK), F32),
            vmem((2, 16, TOK), F32),
            vmem((2, 16, HALF), F32),
            vmem((2, 16, TOK), F32),
            vmem((2, 16, WIDTH), BF16),
            vmem((4, 128, DH), F32),
            dma((4,)),
            dma((4,)),
            dma((4,)),
            dma((HEADS,)),
            dma(()),
            dma((HEADS,)),
            dma(()),
            dma((ZGROUPS,)),
            dma(()),
            dma((ZGROUPS,)),
            dma(()),
            dma((GROUP,)),
            dma(()),
            dma(()),
            dma(()),
        ],
        compiler_params=pltpu.CompilerParams(collective_id=0, has_side_effects=True, vmem_limit_bytes=48 * 1024 * 1024),
    )(offsets, query, key, value, grad_out)


def solution(mesh):
    placed = (P("ctx", None),) * 4 + (P(),)
    return jax.shard_map(
        on_device, mesh=mesh, in_specs=placed, out_specs=(P("ctx", None),) * 3, check_vma=False
    )
```

```python
import jax
import jax.numpy as jnp
from jax import lax
from jax.experimental import pallas as pl
from jax.experimental.pallas import tpu as pltpu
from jax.sharding import PartitionSpec as P

MESH = pl.DeviceIdType.MESH
HEADS = 10
DH = 128
TOK = 256
HALF = TOK // 2
WIDTH = HEADS * DH
GROUP = 16
ZGROUPS = 8
FACTOR = DH**-0.5
SCALE2 = FACTOR * 1.4426950408889634
LOW = -1e30
UNROLL = 2
EARLY = 1
MIDDLE = 2
F32 = jnp.float32
BF16 = jnp.bfloat16

NN = (((1,), (0,)), ((), ()))
NT = (((1,), (1,)), ((), ()))
TN = (((0,), (0,)), ((), ()))


def mm(a, b, dims):
    return lax.dot_general(a, b, dims, preferred_element_type=F32)


def iota(shape, dim):
    return lax.broadcasted_iota(jnp.int32, shape, dim)


def split(x):
    high = x.astype(BF16)
    return high, (x - high.astype(F32)).astype(BF16)


def kernel(
    off_hbm, q_hbm, k_hbm, v_hbm, g_hbm, oq, ok, ov,
    x, px, pr, qr, sb, pb, sc, pc, tt, ts, rs, rb, lx, lr, acc, ls, ws, wx, w2, qp, wd, off,
    ld_sem, off_sem, ready, px_send, px_recv, p1_send, p1_recv, c1_send, c1_recv,
    p2_send, p2_recv, c2_send, c2_recv, p3_send, p3_recv, lx_send, lx_recv,
):
    me = lax.axis_index("ctx")
    core = lax.rem(me, 2)
    z = lax.rem(lax.div(me, 2), 16)
    y = lax.rem(lax.div(me, 32), 4)
    base = lax.div(me, 128) * 128
    zg = lax.div(z, 2)
    zl = lax.rem(z, 2)
    low = zl * 2 + core
    m = y * 4 + low
    mine = (lax.rem(low, 2) * 2 + lax.div(low, 2)) * 4 + y
    owner = mine < HEADS

    def member(j):
        return (base + lax.div(j, 4) * 32 + (zg * 2 + lax.rem(lax.div(j, 2), 2)) * 2 + lax.rem(j, 2),)

    def zpeer(g):
        return (base + y * 32 + (g * 2 + zl) * 2 + core,)

    def owner_of(h):
        k = lax.div(h, 4)
        return lax.rem(h, 4) * 4 + lax.rem(k, 2) * 2 + lax.div(k, 2)

    partner = (me + 1 - 2 * core,)

    def remote(src, dst, send, recv, device):
        return pltpu.make_async_remote_copy(
            src_ref=src, dst_ref=dst, send_sem=send, recv_sem=recv, device_id=device, device_id_type=MESH
        )

    barrier = pltpu.get_barrier_semaphore()
    right = zpeer(lax.rem(zg + 1, ZGROUPS))
    left = zpeer(lax.rem(zg + ZGROUPS - 1, ZGROUPS))
    pl.semaphore_signal(barrier, inc=1, device_id=right, device_id_type=MESH)
    pl.semaphore_signal(barrier, inc=1, device_id=left, device_id_type=MESH)

    @pl.loop(1, GROUP)
    def _(d):
        pl.semaphore_signal(barrier, inc=1, device_id=member(lax.rem(m + d, GROUP)), device_id_type=MESH)

    off_load = pltpu.make_async_copy(off_hbm, off, off_sem)
    off_load.start()
    loads = [
        pltpu.make_async_copy(ref, x.at[i], ld_sem.at[i]) for i, ref in enumerate((q_hbm, k_hbm, v_hbm, g_hbm))
    ]
    for i in (1, 2, 0, 3):
        loads[i].start()

    def pass_on(stage):
        @pl.when(owner)
        def _():
            if stage > 0:
                pl.semaphore_wait(ready.at[2 * stage - 2], 1)
                pl.semaphore_wait(ready.at[2 * stage - 1], 1)
            if stage < 3:
                pl.semaphore_signal(ready.at[2 * stage], inc=1, device_id=right, device_id_type=MESH)
                pl.semaphore_signal(ready.at[2 * stage + 1], inc=1, device_id=left, device_id_type=MESH)

    sb[...] = jnp.zeros_like(sb)
    sc[...] = jnp.zeros_like(sc)
    rb[...] = jnp.zeros_like(rb)
    rs[...] = jnp.zeros_like(rs)
    ls[...] = jnp.zeros_like(ls)
    perm_row = iota((TOK, TOK), 0)
    perm_to = jnp.where(perm_row < HALF, 2 * perm_row, 2 * perm_row - (TOK - 1))
    perm = (iota((TOK, TOK), 1) == perm_to).astype(F32).astype(BF16)
    block = lax.div(iota((16, WIDTH), 1), DH) == iota((16, WIDTH), 0)
    lane_head = lax.div(iota((8, WIDTH), 1), DH)
    row16 = iota((16, TOK), 0)
    lane16 = iota((16, TOK), 1)

    off_load.wait()
    off_lane = jnp.zeros((8, WIDTH), jnp.int32)
    off0 = jnp.zeros((16, TOK), jnp.int32)
    off1 = jnp.zeros((16, TOK), jnp.int32)
    for h in range(HEADS):
        off_lane = jnp.where(lane_head == h, off[0, h], off_lane)
        off0 = jnp.where(row16 == h, off[0, h], off0)
        off1 = jnp.where(row16 == h, off[1, h], off1)
    sel_wide = (lane16 == off1).astype(F32).astype(BF16)
    row_in_pair = lax.rem(off1, 2) == off0
    key_in_pair = lax.rem(lane16, 2) == off0
    both = jnp.logical_and(row_in_pair, key_in_pair)
    weight_wide = jnp.where(both, 2.0, 1.0)
    off_wide = off_lane[0:1, :] > 0

    def pack_pair(i):
        parts = mm(perm, x[i], NN)
        px[i] = jnp.where(off_wide, parts[HALF:], parts[:HALF]).astype(BF16)

    pair_copies = [remote(px.at[i], pr.at[i], px_send.at[i], px_recv.at[i], partner) for i in range(4)]

    def rows_of(j):
        return pl.ds(pl.multiple_of(8 * j, 8), 8)

    def to_owner(src, dst, send, recv, h):
        return remote(src.at[rows_of(h)], dst.at[rows_of(m)], send.at[h], recv, member(owner_of(h)))

    def send_to_owners(src, dst, send, recv):
        @pl.loop(0, HEADS)
        def _(h):
            @pl.when(owner_of(h) != m)
            def _():
                to_owner(src, dst, send, recv, h).start()

            @pl.when(owner_of(h) == m)
            def _():
                pltpu.make_async_copy(src.at[rows_of(h)], dst.at[rows_of(m)], recv).start()

    def wait_sent(src, dst, send, recv):
        @pl.loop(0, HEADS)
        def _(h):
            @pl.when(owner_of(h) != m)
            def _():
                to_owner(src, dst, send, recv, h).wait_send()

    loads[1].wait()
    pack_pair(1)
    loads[2].wait()
    pack_pair(2)

    pl.semaphore_wait(barrier, GROUP + 1)
    pass_on(0)
    pair_copies[1].start()
    pair_copies[2].start()

    loads[0].wait()
    loads[3].wait()
    for i in range(4):
        picked = jnp.where(block, mm(sel_wide, x[i], NN), 0.0)
        qr[i] = picked.astype(BF16)
        for h in range(HEADS):
            sb[8 * h + i : 8 * h + i + 1, :] = picked[h : h + 1, h * DH : (h + 1) * DH]
    send_to_owners(sb, pb, p1_send, p1_recv)

    s_own = mm(qr[0], x[1], NT) * SCALE2
    x_own = mm(qr[3], x[2], NT)
    pair_copies[1].wait_recv()
    pair_copies[2].wait_recv()
    s_cross = jnp.where(row_in_pair[:, :HALF], mm(qr[0], pr[1], NT) * SCALE2, LOW)
    x_cross = mm(qr[3], pr[2], NT)
    peak = jnp.maximum(jnp.max(s_own, 1, keepdims=True), jnp.max(s_cross, 1, keepdims=True))
    e_own = jnp.exp2(s_own - peak) * weight_wide
    e_cross = jnp.exp2(s_cross - peak)
    total = jnp.sum(e_own, 1, keepdims=True) + jnp.sum(e_cross, 1, keepdims=True)
    blend = jnp.sum(e_own * x_own, 1, keepdims=True) + jnp.sum(e_cross * x_cross, 1, keepdims=True)
    lane128 = iota((16, DH), 1)
    here = lane128 == zg * GROUP + m
    wide_lse = jnp.where(here, peak + jnp.log2(total), 0.0)
    wide_delta = jnp.where(here, blend / total, 0.0)
    for h in range(HEADS):
        sc[8 * h : 8 * h + 1, :] = wide_lse[h : h + 1, :]
        sc[8 * h + 1 : 8 * h + 2, :] = wide_delta[h : h + 1, :]
    send_to_owners(sc, pc, c1_send, c1_recv)
    ws[0] = s_own
    ws[1] = x_own
    wx[0] = s_cross
    wx[1] = x_cross
    pass_on(1)
    pack_pair(0)
    pair_copies[0].start()
    pack_pair(3)
    pair_copies[3].start()
    pass_on(2)

    lane_row = iota((1, TOK), 1)
    parity_lane = lax.rem(lane_row, 2)
    parity_sub = lax.rem(iota((1, 8, TOK), 1), 2)
    parity_both = lax.rem(iota((1, 8, TOK), 2), 2)

    def total_of(a):
        return jnp.sum(jnp.sum(a, 0), 0, keepdims=True)

    def peak_of(a):
        return jnp.max(jnp.max(a, 0), 0, keepdims=True)

    def attend(h):
        hs = pl.ds(pl.multiple_of(h * DH, DH), DH)
        qh = x[0, :, hs]
        gh = x[3, :, hs]
        kh = x[1, :, hs]
        vh = x[2, :, hs]
        kx = pr[1, :, hs]
        vx = pr[2, :, hs]
        chosen = parity_lane == off[0, h]
        keep = jnp.where(lane_row == off[1, h], 0.0, 1.0)
        weight = jnp.where(jnp.logical_and(parity_sub == off[0, h], parity_both == off[0, h]), 2.0, 1.0)
        s0 = (mm(kh, qh, NT) * SCALE2).reshape(TOK // 8, 8, TOK)
        s1 = (mm(kx, qh, NT) * SCALE2 + jnp.where(chosen, 0.0, LOW)).reshape(HALF // 8, 8, TOK)
        x0 = mm(vh, gh, NT).reshape(TOK // 8, 8, TOK)
        x1 = mm(vx, gh, NT).reshape(HALF // 8, 8, TOK)
        top = jnp.maximum(peak_of(s0), peak_of(s1))
        e0 = jnp.exp2(s0 - top) * weight
        e1 = jnp.exp2(s1 - top)
        tot = total_of(e0) + total_of(e1)
        num = total_of(e0 * x0) + total_of(e1 * x1)
        inv = 1.0 / tot
        delta = num * inv
        ls[0, pl.ds(h, 1), :] = jnp.where(keep > 0, top + jnp.log2(tot), -LOW)
        ls[1, pl.ds(h, 1), :] = delta
        gain = inv * keep
        slope = gain * FACTOR
        p0 = e0 * gain
        d0 = ((e0 * slope) * (x0 - delta)).reshape(TOK, TOK).astype(BF16)
        d1 = ((e1 * slope) * (x1 - delta)).reshape(HALF, TOK).astype(BF16)
        acc[2, :, hs] = mm(p0.reshape(TOK, TOK).astype(BF16), gh, NN)
        acc[1, :, hs] = mm(d0, qh, NN)
        acc[0, :, hs] = mm(d0, kh, TN) + mm(d1, kx, TN)

    @pl.loop(0, EARLY)
    def _(j):
        for u in range(UNROLL):
            attend(j * UNROLL + u)

    def to_zpeer(src, send, recv, d):
        return remote(src.at[zg], src.at[zg], send.at[d], recv, zpeer(lax.rem(zg + d, ZGROUPS)))

    pass_on(3)

    @pl.when(owner)
    def _():
        pltpu.make_async_copy(pb, pb, p1_recv).wait()
        for i in range(4):
            tt[zg, i] = pb[pl.ds(i, GROUP, stride=8), :].astype(BF16)

        @pl.loop(1, ZGROUPS)
        def _(d):
            to_zpeer(tt, p2_send, p2_recv, d).start()

    @pl.loop(EARLY, MIDDLE)
    def _(j):
        for u in range(UNROLL):
            attend(j * UNROLL + u)

    @pl.when(owner)
    def _():
        pltpu.make_async_copy(pc, pc, c1_recv).wait()
        for i in range(2):
            ts[zg, i : i + 1, :] = jnp.sum(pc[pl.ds(i, GROUP, stride=8), :], 0, keepdims=True)

        @pl.loop(1, ZGROUPS)
        def _(d):
            to_zpeer(ts, c2_send, c2_recv, d).start()

    @pl.loop(MIDDLE, HEADS // UNROLL)
    def _(j):
        for u in range(UNROLL):
            attend(j * UNROLL + u)

    perm_t = jnp.where(iota((TOK, TOK), 1) < HALF, 2 * iota((TOK, TOK), 1), 2 * iota((TOK, TOK), 1) - (TOK - 1))
    perm_t = (iota((TOK, TOK), 0) == perm_t).astype(F32).astype(BF16)
    for i in range(2):
        value = ls[i]
        high, rest = split(value)
        mid, least = split(value - high.astype(F32))
        moved = mm(high, perm_t, NN) + (mm(mid, perm_t, NN) + mm(least, perm_t, NN))
        lx[i] = jnp.where(off0[:, :HALF] > 0, moved[:, HALF:], moved[:, :HALF])
    stat_copy = remote(lx, lr, lx_send, lx_recv, partner)
    stat_copy.start()

    pair_copies[0].wait_recv()
    pair_copies[3].wait_recv()
    lane_pair = iota((16, HALF), 1)
    sel_pair = jnp.logical_and(row_in_pair[:, :HALF], lane_pair == lax.div(off1[:, :HALF], 2))
    sel_pair = sel_pair.astype(F32).astype(BF16)
    qp[0] = jnp.where(block, mm(sel_pair, pr[0], NN), 0.0).astype(BF16)
    qp[1] = jnp.where(block, mm(sel_pair, pr[3], NN), 0.0).astype(BF16)
    w2[0] = jnp.where(both, mm(qp[0], x[1], NT) * SCALE2, LOW)
    w2[1] = mm(qp[1], x[2], NT)

    stat_copy.wait_recv()

    def cross(h):
        hs = pl.ds(pl.multiple_of(h * DH, DH), DH)
        kh = x[1, :, hs]
        vh = x[2, :, hs]
        qx = pr[0, :, hs]
        gx = pr[3, :, hs]
        lse = lr[0, pl.ds(h, 1), :]
        delta = lr[1, pl.ds(h, 1), :]
        s2 = (mm(kh, qx, NT) * SCALE2).reshape(TOK // 8, 8, HALF)
        x2 = mm(vh, gx, NT).reshape(TOK // 8, 8, HALF)
        p2 = jnp.exp2(jnp.where(parity_sub[:, :, :HALF] == off[0, h], s2 - lse, LOW))
        d2 = ((p2 * FACTOR) * (x2 - delta)).reshape(TOK, HALF).astype(BF16)
        acc[2, :, hs] += mm(p2.reshape(TOK, HALF).astype(BF16), gx, NN)
        acc[1, :, hs] += mm(d2, qx, NN)

    @pl.loop(0, HEADS // UNROLL)
    def _(j):
        for u in range(UNROLL):
            cross(j * UNROLL + u)

    def to_member(d):
        j = lax.rem(m + d, GROUP)
        return remote(rs.at[rows_of(j)], rb.at[rows_of(mine)], p3_send.at[d], p3_recv, member(j))

    @pl.when(owner)
    def _():
        seven = pl.ds(0, ZGROUPS - 1)
        pltpu.make_async_copy(tt.at[seven], tt.at[seven], p2_recv).wait()
        pltpu.make_async_copy(ts.at[seven], ts.at[seven], c2_recv).wait()
        qw, kw, vw, gw = [tt[:, i].reshape(128, DH) for i in range(4)]
        stat = jnp.sum(ts[...], 0)
        lse_lp, delta_lp = stat[0:1], stat[1:2]
        s = mm(kw, qw, NT) * SCALE2
        xx = mm(vw, gw, NT)
        top = jnp.max(s, 0, keepdims=True)
        e = jnp.exp2(s - top)
        tot = jnp.sum(e, 0, keepdims=True)
        num = jnp.sum(e * xx, 0, keepdims=True)
        peak = jnp.maximum(top, lse_lp)
        c_w = jnp.exp2(top - peak)
        c_lp = jnp.exp2(lse_lp - peak)
        all_tot = tot * c_w + c_lp
        lse = peak + jnp.log2(all_tot)
        delta = (num * c_w + delta_lp * c_lp) / all_tot
        p = e * (c_w / all_tot)
        ds = ((p * FACTOR) * (xx - delta)).astype(BF16)
        wd[0] = mm(ds, kw, TN)
        wd[1] = mm(ds, qw, NN)
        wd[2] = mm(p.astype(BF16), gw, NN)
        own = pl.ds(pl.multiple_of(zg * GROUP, GROUP), GROUP)
        for i in range(3):
            rs[pl.ds(i, GROUP, stride=8), :] = wd[i, own, :]
        rs[pl.ds(3, GROUP, stride=8), :] = jnp.broadcast_to(lse, (GROUP, DH))
        rs[pl.ds(4, GROUP, stride=8), :] = jnp.broadcast_to(delta, (GROUP, DH))

        @pl.loop(1, GROUP)
        def _(d):
            to_member(d).start()

        pltpu.make_async_copy(rs.at[rows_of(m)], rb.at[rows_of(mine)], p3_recv).start()

    got = pl.ds(0, 8 * HEADS)
    pltpu.make_async_copy(rb.at[got], rb.at[got], p3_recv).wait()

    all_lse = rb[pl.ds(3, 16, stride=8), :]
    all_delta = rb[pl.ds(4, 16, stride=8), :]
    there = lane128 == zg * GROUP + m + 1 - 2 * core

    def at(mask, value):
        return jnp.sum(jnp.where(mask, value, 0.0), 1, keepdims=True)

    lse_r, delta_r = at(here, all_lse), at(here, all_delta)
    lse_f, delta_f = at(there, all_lse), at(there, all_delta)
    p_own = jnp.exp2(ws[0] - lse_r) * weight_wide
    d_own = ((p_own * FACTOR) * (ws[1] - delta_r)).astype(BF16)
    p_cross = jnp.exp2(wx[0] - lse_r)
    d_cross = ((p_cross * FACTOR) * (wx[1] - delta_r)).astype(BF16)
    p_far = jnp.exp2(w2[0] - lse_f)
    d_far = ((p_far * FACTOR) * (w2[1] - delta_f)).astype(BF16)

    def spread(i):
        row = rb[pl.ds(i, 16, stride=8), :]
        return jnp.where(block, jnp.concatenate([row] * HEADS, axis=1), 0.0)

    dq_row = jnp.where(block, mm(d_own, x[1], NN) + mm(d_cross, pr[1], NN), 0.0) + spread(0)
    sel = sel_wide
    fixes = (
        (oq, 0, jnp.concatenate([sel, sel], 0), jnp.concatenate(split(dq_row), 0)),
        (ok, 1, jnp.concatenate([d_own, d_far, sel, sel], 0), jnp.concatenate([qr[0], qp[0], *split(spread(1))], 0)),
        (
            ov,
            2,
            jnp.concatenate([p_own.astype(BF16), p_far.astype(BF16), sel, sel], 0),
            jnp.concatenate([qr[3], qp[1], *split(spread(2))], 0),
        ),
    )
    stores = []
    for ref, i, left, right in fixes:
        ref[...] = (acc[i] + mm(left, right, TN)).astype(BF16)
    for copy in pair_copies:
        copy.wait_send()
    stat_copy.wait_send()
    wait_sent(sb, pb, p1_send, p1_recv)
    wait_sent(sc, pc, c1_send, c1_recv)

    @pl.when(owner)
    def _():
        @pl.loop(1, ZGROUPS)
        def _(d):
            to_zpeer(tt, p2_send, p2_recv, d).wait_send()
            to_zpeer(ts, c2_send, c2_recv, d).wait_send()

        @pl.loop(1, GROUP)
        def _(d):
            to_member(d).wait_send()


def on_device(query, key, value, grad_out, offsets):
    shape = jax.ShapeDtypeStruct((TOK, WIDTH), BF16)
    vmem = pltpu.VMEM
    dma = pltpu.SemaphoreType.DMA
    return pl.pallas_call(
        kernel,
        out_shape=(shape, shape, shape),
        in_specs=[pl.BlockSpec(memory_space=pltpu.MemorySpace.HBM)] * 5,
        out_specs=(pl.BlockSpec(memory_space=vmem),) * 3,
        scratch_shapes=[
            vmem((4, TOK, WIDTH), BF16),
            vmem((4, HALF, WIDTH), BF16),
            vmem((4, HALF, WIDTH), BF16),
            vmem((4, 16, WIDTH), BF16),
            vmem((8 * HEADS, DH), F32),
            vmem((8 * GROUP, DH), F32),
            vmem((8 * HEADS, DH), F32),
            vmem((8 * GROUP, DH), F32),
            vmem((ZGROUPS, 4, GROUP, DH), BF16),
            vmem((ZGROUPS, 2, DH), F32),
            vmem((8 * GROUP, DH), F32),
            vmem((8 * 16, DH), F32),
            vmem((2, 16, HALF), F32),
            vmem((2, 16, HALF), F32),
            vmem((3, TOK, WIDTH), F32),
            vmem((2, 16, TOK), F32),
            vmem((2, 16, TOK), F32),
            vmem((2, 16, HALF), F32),
            vmem((2, 16, TOK), F32),
            vmem((2, 16, WIDTH), BF16),
            vmem((3, 128, DH), F32),
            pltpu.SMEM((2, HEADS), jnp.int32),
            dma((4,)),
            dma(()),
            pltpu.SemaphoreType.REGULAR((6,)),
            dma((4,)),
            dma((4,)),
            dma((HEADS,)),
            dma(()),
            dma((HEADS,)),
            dma(()),
            dma((ZGROUPS,)),
            dma(()),
            dma((ZGROUPS,)),
            dma(()),
            dma((GROUP,)),
            dma(()),
            dma(()),
            dma(()),
        ],
        compiler_params=pltpu.CompilerParams(collective_id=0, has_side_effects=True, vmem_limit_bytes=48 * 1024 * 1024),
    )(*[pltpu.with_memory_space_constraint(a, pltpu.MemorySpace.HBM) for a in (offsets, query, key, value, grad_out)])


def solution(mesh):
    placed = (P("ctx", None),) * 4 + (P(),)
    return jax.shard_map(
        on_device, mesh=mesh, in_specs=placed, out_specs=(P("ctx", None),) * 3, check_vma=False
    )
```

```python
import jax
import jax.numpy as jnp
from jax import lax
from jax.experimental import pallas as pl
from jax.experimental.pallas import tpu as pltpu
from jax.sharding import PartitionSpec as P

MESH = pl.DeviceIdType.MESH
HEADS = 10
DH = 128
TOK = 256
HALF = TOK // 2
WIDTH = HEADS * DH
GROUP = 16
ZGROUPS = 8
FACTOR = DH**-0.5
SCALE2 = FACTOR * 1.4426950408889634
LOW = -1e30
PAIRS = HEADS // 2
CROSS_FIRST = 3
EARLY = 1
F32 = jnp.float32
BF16 = jnp.bfloat16

NN = (((1,), (0,)), ((), ()))
NT = (((1,), (1,)), ((), ()))
TN = (((0,), (0,)), ((), ()))


def mm(a, b, dims):
    return lax.dot_general(a, b, dims, preferred_element_type=F32)


def iota(shape, dim):
    return lax.broadcasted_iota(jnp.int32, shape, dim)


def split(x):
    high = x.astype(BF16)
    return high, (x - high.astype(F32)).astype(BF16)


def kernel(
    off_hbm, q_hbm, k_hbm, v_hbm, g_hbm, acc, left, fix,
    x, px, pr, qr, sb, pb, sc, pc, tt, ts, rs, rb, lx, lr, ls, ws, wx, w2, qp, wd, off,
    ld_sem, off_sem, ready, px_send, px_recv, p1_send, p1_recv, c1_send, c1_recv,
    p2_send, p2_recv, c2_send, c2_recv, p3_send, p3_recv, lx_send, lx_recv,
):
    me = lax.axis_index("ctx")
    core = lax.rem(me, 2)
    z = lax.rem(lax.div(me, 2), 16)
    y = lax.rem(lax.div(me, 32), 4)
    base = lax.div(me, 128) * 128
    zg = lax.div(z, 2)
    zl = lax.rem(z, 2)
    low = zl * 2 + core
    m = y * 4 + low
    mine = (lax.rem(low, 2) * 2 + lax.div(low, 2)) * 4 + y
    owner = mine < HEADS

    def member(j):
        return (base + lax.div(j, 4) * 32 + (zg * 2 + lax.rem(lax.div(j, 2), 2)) * 2 + lax.rem(j, 2),)

    def zpeer(g):
        return (base + y * 32 + (g * 2 + zl) * 2 + core,)

    def owner_of(h):
        k = lax.div(h, 4)
        return lax.rem(h, 4) * 4 + lax.rem(k, 2) * 2 + lax.div(k, 2)

    partner = (me + 1 - 2 * core,)

    def remote(src, dst, send, recv, device):
        return pltpu.make_async_remote_copy(
            src_ref=src, dst_ref=dst, send_sem=send, recv_sem=recv, device_id=device, device_id_type=MESH
        )

    off_load = pltpu.make_async_copy(off_hbm, off, off_sem)
    off_load.start()
    loads = [
        pltpu.make_async_copy(ref, x.at[i], ld_sem.at[i]) for i, ref in enumerate((q_hbm, k_hbm, v_hbm, g_hbm))
    ]
    for i in (1, 2, 0, 3):
        loads[i].start()

    barrier = pltpu.get_barrier_semaphore()
    upper = zpeer(lax.rem(zg + 1, ZGROUPS))
    lower = zpeer(lax.rem(zg + ZGROUPS - 1, ZGROUPS))
    pl.semaphore_signal(barrier, inc=1, device_id=upper, device_id_type=MESH)
    pl.semaphore_signal(barrier, inc=1, device_id=lower, device_id_type=MESH)

    @pl.loop(1, GROUP)
    def _(d):
        pl.semaphore_signal(barrier, inc=1, device_id=member(lax.rem(m + d, GROUP)), device_id_type=MESH)

    def pass_on(stage):
        @pl.when(owner)
        def _():
            if stage > 0:
                pl.semaphore_wait(ready.at[2 * stage - 2], 1)
                pl.semaphore_wait(ready.at[2 * stage - 1], 1)
            if stage < 3:
                pl.semaphore_signal(ready.at[2 * stage], inc=1, device_id=upper, device_id_type=MESH)
                pl.semaphore_signal(ready.at[2 * stage + 1], inc=1, device_id=lower, device_id_type=MESH)

    sb[...] = jnp.zeros_like(sb)
    sc[...] = jnp.zeros_like(sc)
    rb[...] = jnp.zeros_like(rb)
    rs[...] = jnp.zeros_like(rs)
    ls[...] = jnp.zeros_like(ls)
    perm_row = iota((TOK, TOK), 0)
    perm_to = jnp.where(perm_row < HALF, 2 * perm_row, 2 * perm_row - (TOK - 1))
    perm = (iota((TOK, TOK), 1) == perm_to).astype(F32).astype(BF16)
    block = lax.div(iota((16, WIDTH), 1), DH) == iota((16, WIDTH), 0)
    lane_head = lax.div(iota((8, WIDTH), 1), DH)
    row16 = iota((16, TOK), 0)
    lane16 = iota((16, TOK), 1)

    off_load.wait()
    off_lane = jnp.zeros((8, WIDTH), jnp.int32)
    off0 = jnp.zeros((16, TOK), jnp.int32)
    off1 = jnp.zeros((16, TOK), jnp.int32)
    for h in range(HEADS):
        off_lane = jnp.where(lane_head == h, off[0, h], off_lane)
        off0 = jnp.where(row16 == h, off[0, h], off0)
        off1 = jnp.where(row16 == h, off[1, h], off1)
    sel_wide = (lane16 == off1).astype(F32).astype(BF16)
    row_in_pair = lax.rem(off1, 2) == off0
    key_in_pair = lax.rem(lane16, 2) == off0
    both = jnp.logical_and(row_in_pair, key_in_pair)
    weight_wide = jnp.where(both, 2.0, 1.0)
    off_wide = off_lane[0:1, :] > 0

    def pack_pair(i):
        parts = mm(perm, x[i], NN)
        px[i] = jnp.where(off_wide, parts[HALF:], parts[:HALF]).astype(BF16)

    pair_copies = [remote(px.at[i], pr.at[i], px_send.at[i], px_recv.at[i], partner) for i in range(4)]

    def rows_of(j):
        return pl.ds(pl.multiple_of(8 * j, 8), 8)

    def to_owner(src, dst, send, recv, h):
        return remote(src.at[rows_of(h)], dst.at[rows_of(m)], send.at[h], recv, member(owner_of(h)))

    def send_to_owners(src, dst, send, recv):
        @pl.loop(0, HEADS)
        def _(h):
            @pl.when(owner_of(h) != m)
            def _():
                to_owner(src, dst, send, recv, h).start()

            @pl.when(owner_of(h) == m)
            def _():
                pltpu.make_async_copy(src.at[rows_of(h)], dst.at[rows_of(m)], recv).start()

    def wait_sent(src, dst, send, recv):
        @pl.loop(0, HEADS)
        def _(h):
            @pl.when(owner_of(h) != m)
            def _():
                to_owner(src, dst, send, recv, h).wait_send()

    loads[1].wait()
    pack_pair(1)
    pl.semaphore_wait(barrier, GROUP + 1)
    pass_on(0)
    pair_copies[1].start()
    loads[2].wait()
    pack_pair(2)
    pair_copies[2].start()

    loads[0].wait()
    loads[3].wait()
    for i in range(4):
        picked = jnp.where(block, mm(sel_wide, x[i], NN), 0.0)
        qr[i] = picked.astype(BF16)
        for h in range(HEADS):
            sb[8 * h + i : 8 * h + i + 1, :] = picked[h : h + 1, h * DH : (h + 1) * DH]
    send_to_owners(sb, pb, p1_send, p1_recv)

    s_own = mm(qr[0], x[1], NT) * SCALE2
    x_own = mm(qr[3], x[2], NT)
    pair_copies[1].wait_recv()
    pair_copies[2].wait_recv()
    pass_on(1)
    s_cross = jnp.where(row_in_pair[:, :HALF], mm(qr[0], pr[1], NT) * SCALE2, LOW)
    x_cross = mm(qr[3], pr[2], NT)
    peak = jnp.maximum(jnp.max(s_own, 1, keepdims=True), jnp.max(s_cross, 1, keepdims=True))
    e_own = jnp.exp2(s_own - peak) * weight_wide
    e_cross = jnp.exp2(s_cross - peak)
    total = jnp.sum(e_own, 1, keepdims=True) + jnp.sum(e_cross, 1, keepdims=True)
    blend = jnp.sum(e_own * x_own, 1, keepdims=True) + jnp.sum(e_cross * x_cross, 1, keepdims=True)
    lane128 = iota((16, DH), 1)
    here = lane128 == zg * GROUP + m
    wide_lse = jnp.where(here, peak + jnp.log2(total), 0.0)
    wide_delta = jnp.where(here, blend / total, 0.0)
    for h in range(HEADS):
        sc[8 * h : 8 * h + 1, :] = wide_lse[h : h + 1, :]
        sc[8 * h + 1 : 8 * h + 2, :] = wide_delta[h : h + 1, :]
    send_to_owners(sc, pc, c1_send, c1_recv)
    ws[0] = s_own
    ws[1] = x_own
    wx[0] = s_cross
    wx[1] = x_cross
    pack_pair(0)
    pair_copies[0].start()
    pack_pair(3)
    pair_copies[3].start()
    pass_on(2)

    lane_row = iota((1, TOK), 1)
    parity_lane = lax.rem(lane_row, 2)
    parity_sub = lax.rem(iota((1, 8, TOK), 1), 2)
    parity_both = lax.rem(iota((1, 8, TOK), 2), 2)

    def total_of(a):
        return jnp.sum(jnp.sum(a, 0), 0, keepdims=True)

    def peak_of(a):
        return jnp.max(jnp.max(a, 0), 0, keepdims=True)

    def lanes(h):
        return pl.ds(pl.multiple_of(h * DH, DH), DH)

    def two_lanes(j):
        return pl.ds(pl.multiple_of(j * 2 * DH, 2 * DH), 2 * DH)

    def diagonal(a, b):
        blank = jnp.zeros_like(a)
        return jnp.concatenate([jnp.concatenate([a, blank], 1), jnp.concatenate([blank, b], 1)], 0)

    def attend(h):
        hs = lanes(h)
        qh = x[0, :, hs]
        gh = x[3, :, hs]
        kh = x[1, :, hs]
        vh = x[2, :, hs]
        kx = pr[1, :, hs]
        vx = pr[2, :, hs]
        chosen = parity_lane == off[0, h]
        keep = jnp.where(lane_row == off[1, h], 0.0, 1.0)
        weight = jnp.where(jnp.logical_and(parity_sub == off[0, h], parity_both == off[0, h]), 2.0, 1.0)
        s0 = (mm(kh, qh, NT) * SCALE2).reshape(TOK // 8, 8, TOK)
        s1 = (mm(kx, qh, NT) * SCALE2 + jnp.where(chosen, 0.0, LOW)).reshape(HALF // 8, 8, TOK)
        x0 = mm(vh, gh, NT).reshape(TOK // 8, 8, TOK)
        x1 = mm(vx, gh, NT).reshape(HALF // 8, 8, TOK)
        top = jnp.maximum(peak_of(s0), peak_of(s1))
        e0 = jnp.exp2(s0 - top) * weight
        e1 = jnp.exp2(s1 - top)
        tot = total_of(e0) + total_of(e1)
        num = total_of(e0 * x0) + total_of(e1 * x1)
        inv = 1.0 / tot
        delta = num * inv
        ls[0, pl.ds(h, 1), :] = jnp.where(keep > 0, top + jnp.log2(tot), -LOW)
        ls[1, pl.ds(h, 1), :] = delta
        gain = inv * keep
        slope = gain * FACTOR
        p0 = e0 * gain
        d0 = ((e0 * slope) * (x0 - delta)).reshape(TOK, TOK).astype(BF16)
        d1 = ((e1 * slope) * (x1 - delta)).reshape(HALF, TOK).astype(BF16)
        acc[2, :, hs] = mm(p0.reshape(TOK, TOK).astype(BF16), gh, NN)
        acc[1, :, hs] = mm(d0, qh, NN)
        return mm(d0, kh, TN), d1, kx

    def attend_two(j):
        own_a, far_a, kx_a = attend(2 * j)
        own_b, far_b, kx_b = attend(2 * j + 1)
        far = mm(jnp.concatenate([far_a, far_b], 0), diagonal(kx_a, kx_b), TN)
        acc[0, :, two_lanes(j)] = jnp.concatenate([own_a, own_b], 1) + far

    def to_zpeer(src, send, recv, d):
        return remote(src.at[zg], src.at[zg], send.at[d], recv, zpeer(lax.rem(zg + d, ZGROUPS)))

    @pl.when(owner)
    def _():
        pltpu.make_async_copy(pb, pb, p1_recv).wait()
        for i in range(4):
            tt[zg, i] = pb[pl.ds(i, GROUP, stride=8), :].astype(BF16)
        for d in (3, 5, 2, 6, 1, 7):
            to_zpeer(tt, p2_send, p2_recv, d).start()

    @pl.loop(0, EARLY)
    def _(j):
        attend_two(j)

    pass_on(3)

    @pl.when(owner)
    def _():
        to_zpeer(tt, p2_send, p2_recv, 4).start()
        pltpu.make_async_copy(pc, pc, c1_recv).wait()
        for i in range(2):
            ts[zg, i : i + 1, :] = jnp.sum(pc[pl.ds(i, GROUP, stride=8), :], 0, keepdims=True)
        for d in (4, 3, 5, 2, 6, 1, 7):
            to_zpeer(ts, c2_send, c2_recv, d).start()

    @pl.loop(EARLY, PAIRS)
    def _(j):
        attend_two(j)

    perm_t = jnp.where(iota((TOK, TOK), 1) < HALF, 2 * iota((TOK, TOK), 1), 2 * iota((TOK, TOK), 1) - (TOK - 1))
    perm_t = (iota((TOK, TOK), 0) == perm_t).astype(F32).astype(BF16)
    for i in range(2):
        value = ls[i]
        high, rest = split(value)
        mid, least = split(value - high.astype(F32))
        moved = mm(high, perm_t, NN) + (mm(mid, perm_t, NN) + mm(least, perm_t, NN))
        lx[i] = jnp.where(off0[:, :HALF] > 0, moved[:, HALF:], moved[:, :HALF])
    stat_copy = remote(lx, lr, lx_send, lx_recv, partner)
    stat_copy.start()

    pair_copies[0].wait_recv()
    pair_copies[3].wait_recv()
    stat_copy.wait_recv()

    def cross(h):
        hs = lanes(h)
        qx = pr[0, :, hs]
        gx = pr[3, :, hs]
        lse = lr[0, pl.ds(h, 1), :]
        delta = lr[1, pl.ds(h, 1), :]
        both_in = mm(jnp.concatenate([x[1, :, hs], x[2, :, hs]], 1), diagonal(qx, gx), NT)
        s2 = (both_in[:, :HALF] * SCALE2).reshape(TOK // 8, 8, HALF)
        x2 = both_in[:, HALF:].reshape(TOK // 8, 8, HALF)
        p2 = jnp.exp2(jnp.where(parity_sub[:, :, :HALF] == off[0, h], s2 - lse, LOW))
        d2 = ((p2 * FACTOR) * (x2 - delta)).reshape(TOK, HALF).astype(BF16)
        p2 = p2.reshape(TOK, HALF).astype(BF16)
        both_out = mm(jnp.concatenate([p2, d2], 1), diagonal(gx, qx), NN)
        acc[2, :, hs] += both_out[:, :DH]
        acc[1, :, hs] += both_out[:, DH:]

    def cross_two(j):
        cross(2 * j)
        cross(2 * j + 1)

    @pl.loop(0, CROSS_FIRST)
    def _(j):
        cross_two(j)

    def to_member(d):
        j = lax.rem(m + d, GROUP)
        return remote(rs.at[rows_of(j)], rb.at[rows_of(mine)], p3_send.at[d], p3_recv, member(j))

    @pl.when(owner)
    def _():
        seven = pl.ds(0, ZGROUPS - 1)
        pltpu.make_async_copy(tt.at[seven], tt.at[seven], p2_recv).wait()
        pltpu.make_async_copy(ts.at[seven], ts.at[seven], c2_recv).wait()
        qw, kw, vw, gw = [tt[:, i].reshape(128, DH) for i in range(4)]
        stat = jnp.sum(ts[...], 0)
        lse_lp, delta_lp = stat[0:1], stat[1:2]
        s = mm(kw, qw, NT) * SCALE2
        xx = mm(vw, gw, NT)
        top = jnp.max(s, 0, keepdims=True)
        e = jnp.exp2(s - top)
        tot = jnp.sum(e, 0, keepdims=True)
        num = jnp.sum(e * xx, 0, keepdims=True)
        peak = jnp.maximum(top, lse_lp)
        c_w = jnp.exp2(top - peak)
        c_lp = jnp.exp2(lse_lp - peak)
        all_tot = tot * c_w + c_lp
        lse = peak + jnp.log2(all_tot)
        delta = (num * c_w + delta_lp * c_lp) / all_tot
        p = e * (c_w / all_tot)
        ds = ((p * FACTOR) * (xx - delta)).astype(BF16)
        wd[0] = mm(ds, kw, TN)
        wd[1] = mm(ds, qw, NN)
        wd[2] = mm(p.astype(BF16), gw, NN)
        own = pl.ds(pl.multiple_of(zg * GROUP, GROUP), GROUP)
        for i in range(3):
            rs[pl.ds(i, GROUP, stride=8), :] = wd[i, own, :]
        rs[pl.ds(3, GROUP, stride=8), :] = jnp.broadcast_to(lse, (GROUP, DH))
        rs[pl.ds(4, GROUP, stride=8), :] = jnp.broadcast_to(delta, (GROUP, DH))

        @pl.loop(1, GROUP)
        def _(d):
            to_member(d).start()

        pltpu.make_async_copy(rs.at[rows_of(m)], rb.at[rows_of(mine)], p3_recv).start()

    @pl.loop(CROSS_FIRST, PAIRS)
    def _(j):
        cross_two(j)

    lane_pair = iota((16, HALF), 1)
    sel_pair = jnp.logical_and(row_in_pair[:, :HALF], lane_pair == lax.div(off1[:, :HALF], 2))
    sel_pair = sel_pair.astype(F32).astype(BF16)
    qp[0] = jnp.where(block, mm(sel_pair, pr[0], NN), 0.0).astype(BF16)
    qp[1] = jnp.where(block, mm(sel_pair, pr[3], NN), 0.0).astype(BF16)
    w2[0] = jnp.where(both, mm(qp[0], x[1], NT) * SCALE2, LOW)
    w2[1] = mm(qp[1], x[2], NT)

    for copy in pair_copies:
        copy.wait_send()
    stat_copy.wait_send()
    wait_sent(sb, pb, p1_send, p1_recv)
    wait_sent(sc, pc, c1_send, c1_recv)

    @pl.when(owner)
    def _():
        @pl.loop(1, ZGROUPS)
        def _(d):
            to_zpeer(tt, p2_send, p2_recv, d).wait_send()
            to_zpeer(ts, c2_send, c2_recv, d).wait_send()

        @pl.loop(1, GROUP)
        def _(d):
            to_member(d).wait_send()

    got = pl.ds(0, 8 * HEADS)
    pltpu.make_async_copy(rb.at[got], rb.at[got], p3_recv).wait()

    all_lse = rb[pl.ds(3, 16, stride=8), :]
    all_delta = rb[pl.ds(4, 16, stride=8), :]
    there = lane128 == zg * GROUP + m + 1 - 2 * core

    def at(mask, value):
        return jnp.sum(jnp.where(mask, value, 0.0), 1, keepdims=True)

    lse_r, delta_r = at(here, all_lse), at(here, all_delta)
    lse_f, delta_f = at(there, all_lse), at(there, all_delta)
    p_own = jnp.exp2(ws[0] - lse_r) * weight_wide
    d_own = ((p_own * FACTOR) * (ws[1] - delta_r)).astype(BF16)
    p_cross = jnp.exp2(wx[0] - lse_r)
    d_cross = ((p_cross * FACTOR) * (wx[1] - delta_r)).astype(BF16)
    p_far = jnp.exp2(w2[0] - lse_f)
    d_far = ((p_far * FACTOR) * (w2[1] - delta_f)).astype(BF16)

    def spread(i):
        row = rb[pl.ds(i, 16, stride=8), :]
        return jnp.where(block, jnp.concatenate([row] * HEADS, axis=1), 0.0)

    dq_row = jnp.where(block, mm(d_own, x[1], NN) + mm(d_cross, pr[1], NN), 0.0) + spread(0)
    sel = sel_wide
    blank_left = jnp.zeros((32, TOK), BF16)
    blank_right = jnp.zeros((32, WIDTH), BF16)
    left[0] = jnp.concatenate([sel, sel, blank_left], 0)
    fix[0] = jnp.concatenate([*split(dq_row), blank_right], 0)
    left[1] = jnp.concatenate([d_own, d_far, sel, sel], 0)
    fix[1] = jnp.concatenate([qr[0], qp[0], *split(spread(1))], 0)
    left[2] = jnp.concatenate([p_own.astype(BF16), p_far.astype(BF16), sel, sel], 0)
    fix[2] = jnp.concatenate([qr[3], qp[1], *split(spread(2))], 0)


def finish(acc, left, fix, oq, ok, ov, held, sem):
    stores = []
    for i, ref in enumerate((oq, ok, ov)):
        held[i] = (acc[i] + mm(left[i], fix[i], TN)).astype(BF16)
        stores.append(pltpu.make_async_copy(held.at[i], ref, sem.at[i]))
        stores[i].start()
    for store in stores:
        store.wait()


def on_device(query, key, value, grad_out, offsets):
    shape = jax.ShapeDtypeStruct((TOK, WIDTH), BF16)
    vmem = pltpu.VMEM
    dma = pltpu.SemaphoreType.DMA
    acc, left, fix = pl.pallas_call(
        kernel,
        out_shape=(
            jax.ShapeDtypeStruct((3, TOK, WIDTH), F32),
            jax.ShapeDtypeStruct((3, 64, TOK), BF16),
            jax.ShapeDtypeStruct((3, 64, WIDTH), BF16),
        ),
        in_specs=[pl.BlockSpec(memory_space=pltpu.MemorySpace.HBM)] * 5,
        out_specs=(pl.BlockSpec(memory_space=vmem),) * 3,
        scratch_shapes=[
            vmem((4, TOK, WIDTH), BF16),
            vmem((4, HALF, WIDTH), BF16),
            vmem((4, HALF, WIDTH), BF16),
            vmem((4, 16, WIDTH), BF16),
            vmem((8 * HEADS, DH), F32),
            vmem((8 * GROUP, DH), F32),
            vmem((8 * HEADS, DH), F32),
            vmem((8 * GROUP, DH), F32),
            vmem((ZGROUPS, 4, GROUP, DH), BF16),
            vmem((ZGROUPS, 2, DH), F32),
            vmem((8 * GROUP, DH), F32),
            vmem((8 * 16, DH), F32),
            vmem((2, 16, HALF), F32),
            vmem((2, 16, HALF), F32),
            vmem((2, 16, TOK), F32),
            vmem((2, 16, TOK), F32),
            vmem((2, 16, HALF), F32),
            vmem((2, 16, TOK), F32),
            vmem((2, 16, WIDTH), BF16),
            vmem((3, 128, DH), F32),
            pltpu.SMEM((2, HEADS), jnp.int32),
            dma((4,)),
            dma(()),
            pltpu.SemaphoreType.REGULAR((6,)),
            dma((4,)),
            dma((4,)),
            dma((HEADS,)),
            dma(()),
            dma((HEADS,)),
            dma(()),
            dma((ZGROUPS,)),
            dma(()),
            dma((ZGROUPS,)),
            dma(()),
            dma((GROUP,)),
            dma(()),
            dma(()),
            dma(()),
        ],
        compiler_params=pltpu.CompilerParams(collective_id=0, has_side_effects=True, vmem_limit_bytes=48 * 1024 * 1024),
    )(*[pltpu.with_memory_space_constraint(a, pltpu.MemorySpace.HBM) for a in (offsets, query, key, value, grad_out)])
    return pl.pallas_call(
        finish,
        out_shape=(shape, shape, shape),
        in_specs=[pl.BlockSpec(memory_space=vmem)] * 3,
        out_specs=(pl.BlockSpec(memory_space=pl.ANY),) * 3,
        scratch_shapes=[vmem((3, TOK, WIDTH), BF16), dma((3,))],
        compiler_params=pltpu.CompilerParams(vmem_limit_bytes=8 * 1024 * 1024),
    )(acc, left, fix)


def solution(mesh):
    placed = (P("ctx", None),) * 4 + (P(),)
    return jax.shard_map(
        on_device, mesh=mesh, in_specs=placed, out_specs=(P("ctx", None),) * 3, check_vma=False
    )
```

```python
import jax
import jax.numpy as jnp
from jax import lax
from jax.experimental import pallas as pl
from jax.experimental.pallas import tpu as pltpu
from jax.sharding import PartitionSpec as P

MESH = pl.DeviceIdType.MESH
HEADS = 10
DH = 128
TOK = 256
HALF = TOK // 2
WIDTH = HEADS * DH
GROUP = 16
ZGROUPS = 8
FACTOR = DH**-0.5
SCALE2 = FACTOR * 1.4426950408889634
LOW = -1e30
PAIRS = HEADS // 2
CROSS_FIRST = 3
F32 = jnp.float32
BF16 = jnp.bfloat16

NN = (((1,), (0,)), ((), ()))
NT = (((1,), (1,)), ((), ()))
TN = (((0,), (0,)), ((), ()))


def mm(a, b, dims):
    return lax.dot_general(a, b, dims, preferred_element_type=F32)


def iota(shape, dim):
    return lax.broadcasted_iota(jnp.int32, shape, dim)


def split(x):
    high = x.astype(BF16)
    return high, (x - high.astype(F32)).astype(BF16)


def kernel(
    off_hbm, q_hbm, k_hbm, v_hbm, g_hbm, acc, left, fix,
    x, px, pr, qr, sb, pb, sc, pc, tt, ts, rs, rb, lx, lr, ls, ws, wx, w2, qp, wd, off, sa, sb2, ta, tb, da, db, ua, ub, ea, eb,
    ld_sem, off_sem, ready, px_send, px_recv, p1_send, p1_recv, c1_send, c1_recv,
    p2_send, p2_recv, c2_send, c2_recv, p3_send, p3_recv, lx_send, lx_recv, qp_send, qp_recv,
):
    me = lax.axis_index("ctx")
    core = lax.rem(me, 2)
    z = lax.rem(lax.div(me, 2), 16)
    y = lax.rem(lax.div(me, 32), 4)
    base = lax.div(me, 128) * 128
    zg = lax.div(z, 2)
    zl = lax.rem(z, 2)
    m = y * 4 + zl * 2 + core
    turned = lax.rem(zl + lax.div(zg, 4), 2)
    drift = core * (1 - turned)
    mine = (core * 2 + turned) * 4 + lax.rem(y + 2 * lax.rem(zg, 2) * drift, 4)
    owner = mine < HEADS

    def member(j):
        return (base + lax.div(j, 4) * 32 + (zg * 2 + lax.rem(lax.div(j, 2), 2)) * 2 + lax.rem(j, 2),)

    def zpeer(d):
        g = lax.rem(zg + d, ZGROUPS)
        row = lax.rem(y + 2 * (d % 2) * drift, 4)
        return (base + row * 32 + (g * 2 + lax.rem(turned + lax.div(g, 4), 2)) * 2 + core,)

    def owner_of(h):
        k = lax.div(h, 4)
        row = lax.rem(lax.rem(h, 4) + 2 * lax.rem(zg, 2) * lax.div(k, 2), 4)
        return row * 4 + lax.rem(lax.rem(k, 2) + lax.div(zg, 4), 2) * 2 + lax.div(k, 2)

    partner = (me + 1 - 2 * core,)

    def remote(src, dst, send, recv, device):
        return pltpu.make_async_remote_copy(
            src_ref=src, dst_ref=dst, send_sem=send, recv_sem=recv, device_id=device, device_id_type=MESH
        )

    off_load = pltpu.make_async_copy(off_hbm, off, off_sem)
    off_load.start()
    loads = [
        pltpu.make_async_copy(ref, x.at[i], ld_sem.at[i]) for i, ref in enumerate((q_hbm, k_hbm, v_hbm, g_hbm))
    ]
    for i in (1, 2, 0, 3):
        loads[i].start()

    barrier = pltpu.get_barrier_semaphore()
    upper = zpeer(1)
    lower = zpeer(ZGROUPS - 1)
    upper2 = zpeer(2)
    lower2 = zpeer(ZGROUPS - 2)
    for there in (upper2, lower2, upper, lower):
        pl.semaphore_signal(barrier, inc=1, device_id=there, device_id_type=MESH)

    plane = base + zg * 4
    ys = [lax.rem(y + i, 4) * 32 for i in range(4)]
    zs = [zl * 2, 2 - zl * 2]
    cs = [core, 1 - core]
    for i in range(1, GROUP):
        there = plane + ys[i // 4] + (zs[i // 2 % 2] + cs[i % 2])
        pl.semaphore_signal(barrier, inc=1, device_id=(there,), device_id_type=MESH)

    def near_groups_ready():
        @pl.when(owner)
        def _():
            pl.semaphore_signal(ready.at[0], inc=1, device_id=upper2, device_id_type=MESH)
            pl.semaphore_signal(ready.at[1], inc=1, device_id=lower2, device_id_type=MESH)

    def far_groups_ready():
        @pl.when(owner)
        def _():
            pl.semaphore_wait(ready.at[0], 1)
            pl.semaphore_wait(ready.at[1], 1)

    sb[...] = jnp.zeros_like(sb)
    sc[...] = jnp.zeros_like(sc)
    rb[...] = jnp.zeros_like(rb)
    rs[...] = jnp.zeros_like(rs)
    ls[...] = jnp.zeros_like(ls)
    perm_row = iota((TOK, TOK), 0)
    perm_to = jnp.where(perm_row < HALF, 2 * perm_row, 2 * perm_row - (TOK - 1))
    perm = (iota((TOK, TOK), 1) == perm_to).astype(F32).astype(BF16)
    block = lax.div(iota((16, WIDTH), 1), DH) == iota((16, WIDTH), 0)
    lane_head = lax.div(iota((8, WIDTH), 1), DH)
    row16 = iota((16, TOK), 0)
    lane16 = iota((16, TOK), 1)

    off_load.wait()
    off_lane = jnp.zeros((8, WIDTH), jnp.int32)
    off0 = jnp.zeros((16, TOK), jnp.int32)
    off1 = jnp.zeros((16, TOK), jnp.int32)
    for h in range(HEADS):
        off_lane = jnp.where(lane_head == h, off[0, h], off_lane)
        off0 = jnp.where(row16 == h, off[0, h], off0)
        off1 = jnp.where(row16 == h, off[1, h], off1)
    sel_wide = (lane16 == off1).astype(F32).astype(BF16)
    row_in_pair = lax.rem(off1, 2) == off0
    key_in_pair = lax.rem(lane16, 2) == off0
    both = jnp.logical_and(row_in_pair, key_in_pair)
    weight_wide = jnp.where(both, 2.0, 1.0)
    off_wide = off_lane[0:1, :] > 0

    def pack_pair(i):
        parts = mm(perm, x[i], NN)
        px[i] = jnp.where(off_wide, parts[HALF:], parts[:HALF]).astype(BF16)

    pair_copies = [remote(px.at[i], pr.at[i], px_send.at[i], px_recv.at[i], partner) for i in range(4)]

    def rows_of(j):
        return pl.ds(pl.multiple_of(8 * j, 8), 8)

    def to_owner(src, dst, send, recv, h):
        return remote(src.at[rows_of(h)], dst.at[rows_of(m)], send.at[h], recv, member(owner_of(h)))

    def send_to_owners(src, dst, send, recv):
        @pl.loop(0, HEADS)
        def _(h):
            @pl.when(owner_of(h) != m)
            def _():
                to_owner(src, dst, send, recv, h).start()

            @pl.when(owner_of(h) == m)
            def _():
                pltpu.make_async_copy(src.at[rows_of(h)], dst.at[rows_of(m)], recv).start()

    def wait_sent(src, dst, send, recv):
        @pl.loop(0, HEADS)
        def _(h):
            @pl.when(owner_of(h) != m)
            def _():
                to_owner(src, dst, send, recv, h).wait_send()

    loads[1].wait()
    pack_pair(1)
    loads[2].wait()
    pack_pair(2)
    loads[0].wait()
    loads[3].wait()
    for i in range(4):
        picked = jnp.where(block, mm(sel_wide, x[i], NN), 0.0)
        qr[i] = picked.astype(BF16)
        for h in range(HEADS):
            sb[8 * h + i : 8 * h + i + 1, :] = picked[h : h + 1, h * DH : (h + 1) * DH]

    s_own = mm(qr[0], x[1], NT) * SCALE2
    x_own = mm(qr[3], x[2], NT)
    ws[0] = s_own
    ws[1] = x_own
    lane128 = iota((16, DH), 1)
    token = zg * GROUP + m
    here = lane128 == token
    other = lane128 == token + 1 - 2 * core

    def statistics(s, value, weight, row, at):
        peak = jnp.max(s, 1, keepdims=True)
        e = jnp.exp2(s - peak)
        e = e if weight is None else e * weight
        total = jnp.sum(e, 1, keepdims=True)
        blend = jnp.sum(e * value, 1, keepdims=True)
        lse = jnp.where(at, peak + jnp.log2(total), 0.0)
        delta = jnp.where(at, blend / total, 0.0)
        for h in range(HEADS):
            sc[8 * h + row : 8 * h + row + 1, :] = lse[h : h + 1, :]
            sc[8 * h + row + 1 : 8 * h + row + 2, :] = delta[h : h + 1, :]

    statistics(s_own, x_own, weight_wide, 0, here)

    pl.semaphore_wait(barrier, GROUP + 3)
    near_groups_ready()
    wide_copies = [remote(qr.at[3 * i], qp.at[i], qp_send.at[i], qp_recv.at[i], partner) for i in range(2)]
    for copy in wide_copies:
        copy.start()
    send_to_owners(sb, pb, p1_send, p1_recv)
    pair_copies[1].start()
    pair_copies[2].start()

    for copy in wide_copies:
        copy.wait_recv()
    s_far = jnp.where(both, mm(qp[0], x[1], NT) * SCALE2, LOW)
    x_far = mm(qp[1], x[2], NT)
    statistics(s_far, x_far, None, 2, other)
    send_to_owners(sc, pc, c1_send, c1_recv)
    w2[0] = s_far
    w2[1] = x_far

    pack_pair(0)
    pair_copies[0].start()
    pack_pair(3)
    pair_copies[3].start()

    lane_row = iota((1, TOK), 1)
    parity_lane = lax.rem(lane_row, 2)
    parity_sub = lax.rem(iota((1, 8, TOK), 1), 2)
    parity_both = lax.rem(iota((1, 8, TOK), 2), 2)

    def total_of(a):
        return jnp.sum(jnp.sum(a, 0), 0, keepdims=True)

    def peak_of(a):
        return jnp.max(jnp.max(a, 0), 0, keepdims=True)

    def lanes(h):
        return pl.ds(pl.multiple_of(h * DH, DH), DH)

    def products(h, sx, top_ref):
        hs = lanes(h)
        qh = x[0, :, hs]
        gh = x[3, :, hs]
        s0 = mm(x[1, :, hs], qh, NT) * SCALE2
        s1 = mm(pr[1, :, hs], qh, NT) * SCALE2 + jnp.where(parity_lane == off[0, h], 0.0, LOW)
        sx[0, :TOK, :] = s0
        sx[0, TOK:, :] = s1
        sx[1, :TOK, :] = mm(x[2, :, hs], gh, NT)
        sx[1, TOK:, :] = mm(pr[2, :, hs], gh, NT)
        top = jnp.maximum(peak_of(s0.reshape(TOK // 8, 8, TOK)), peak_of(s1.reshape(HALF // 8, 8, TOK)))
        top_ref[...] = top

    def weigh(h, sx, top_ref, pd):
        top = top_ref[...]
        keep = jnp.where(lane_row == off[1, h], 0.0, 1.0)
        twice = jnp.logical_and(parity_sub == off[0, h], parity_both == off[0, h])
        lifted = top[None] - jnp.where(twice, 1.0, 0.0)
        e0 = jnp.exp2(sx[0, :TOK, :].reshape(TOK // 8, 8, TOK) - lifted)
        e1 = jnp.exp2(sx[0, TOK:, :].reshape(HALF // 8, 8, TOK) - top)
        x0 = sx[1, :TOK, :].reshape(TOK // 8, 8, TOK)
        x1 = sx[1, TOK:, :].reshape(HALF // 8, 8, TOK)
        tot = total_of(e0) + total_of(e1)
        num = total_of(e0 * x0) + total_of(e1 * x1)
        inv = 1.0 / tot
        delta = num * inv
        ls[0, pl.ds(h, 1), :] = jnp.where(keep > 0, top + jnp.log2(tot), -LOW)
        ls[1, pl.ds(h, 1), :] = delta
        gain = inv * keep
        slope = gain * FACTOR
        pd[:TOK, :] = (e0 * gain).reshape(TOK, TOK).astype(BF16)
        pd[TOK : 2 * TOK, :] = ((e0 * slope) * (x0 - delta)).reshape(TOK, TOK).astype(BF16)
        pd[2 * TOK :, :] = ((e1 * slope) * (x1 - delta)).reshape(HALF, TOK).astype(BF16)

    def gather(h, pd):
        hs = lanes(h)
        acc[2, :, hs] = mm(pd[:TOK, :], x[3, :, hs], NN)
        acc[1, :, hs] = mm(pd[TOK : 2 * TOK, :], x[0, :, hs], NN)
        acc[0, :, hs] = mm(pd[TOK : 2 * TOK, :], x[1, :, hs], TN) + mm(pd[2 * TOK :, :], pr[1, :, hs], TN)

    def to_zpeer(src, send, recv, d):
        return remote(src.at[zg], src.at[zg], send.at[d], recv, zpeer(d))

    far_groups_ready()
    @pl.when(owner)
    def _():
        pltpu.make_async_copy(pb, pb, p1_recv).wait()
        for i in range(4):
            tt[zg, i] = pb[pl.ds(i, GROUP, stride=8), :].astype(BF16)
        for d in (4, 3, 5, 2, 6, 1, 7):
            to_zpeer(tt, p2_send, p2_recv, d).start()

    pair_copies[1].wait_recv()
    pair_copies[2].wait_recv()
    products(0, sa, ta)
    weigh(0, sa, ta, da)
    products(1, sb2, tb)
    gather(0, da)
    weigh(1, sb2, tb, db)
    products(2, sa, ta)

    @pl.when(owner)
    def _():
        pltpu.make_async_copy(pc, pc, c1_recv).wait()
        for i in range(4):
            ts[zg, i : i + 1, :] = jnp.sum(pc[pl.ds(i, GROUP, stride=8), :], 0, keepdims=True)
        for d in (4, 3, 5, 2, 6, 1, 7):
            to_zpeer(ts, c2_send, c2_recv, d).start()

    @pl.loop(1, PAIRS)
    def _(j):
        gather(2 * j - 1, db)
        weigh(2 * j, sa, ta, da)
        products(2 * j + 1, sb2, tb)
        gather(2 * j, da)
        weigh(2 * j + 1, sb2, tb, db)
        products(jnp.minimum(2 * j + 2, HEADS - 1), sa, ta)

    gather(HEADS - 1, db)

    perm_t = jnp.where(iota((TOK, TOK), 1) < HALF, 2 * iota((TOK, TOK), 1), 2 * iota((TOK, TOK), 1) - (TOK - 1))
    perm_t = (iota((TOK, TOK), 0) == perm_t).astype(F32).astype(BF16)
    for i in range(2):
        value = ls[i]
        high, rest = split(value)
        mid, least = split(value - high.astype(F32))
        moved = mm(high, perm_t, NN) + (mm(mid, perm_t, NN) + mm(least, perm_t, NN))
        lx[i] = jnp.where(off0[:, :HALF] > 0, moved[:, HALF:], moved[:, :HALF])
    stat_copy = remote(lx, lr, lx_send, lx_recv, partner)
    stat_copy.start()

    pair_copies[0].wait_recv()
    pair_copies[3].wait_recv()
    stat_copy.wait_recv()

    def cross_products(h, sx):
        hs = lanes(h)
        sx[0] = mm(x[1, :, hs], pr[0, :, hs], NT) * SCALE2
        sx[1] = mm(x[2, :, hs], pr[3, :, hs], NT)

    def cross_weigh(h, sx, pd):
        lse = lr[0, pl.ds(h, 1), :]
        delta = lr[1, pl.ds(h, 1), :]
        s2 = sx[0].reshape(TOK // 8, 8, HALF)
        x2 = sx[1].reshape(TOK // 8, 8, HALF)
        p2 = jnp.exp2(jnp.where(parity_sub[:, :, :HALF] == off[0, h], s2 - lse, LOW))
        pd[0] = p2.reshape(TOK, HALF).astype(BF16)
        pd[1] = ((p2 * FACTOR) * (x2 - delta)).reshape(TOK, HALF).astype(BF16)

    def cross_gather(h, pd):
        hs = lanes(h)
        acc[2, :, hs] += mm(pd[0], pr[3, :, hs], NN)
        acc[1, :, hs] += mm(pd[1], pr[0, :, hs], NN)

    def cross_two(j):
        cross_gather(2 * j - 1, eb)
        cross_weigh(2 * j, ua, ea)
        cross_products(2 * j + 1, ub)
        cross_gather(2 * j, ea)
        cross_weigh(2 * j + 1, ub, eb)
        cross_products(jnp.minimum(2 * j + 2, HEADS - 1), ua)

    cross_products(0, ua)
    cross_weigh(0, ua, ea)
    cross_products(1, ub)
    cross_gather(0, ea)
    cross_weigh(1, ub, eb)
    cross_products(2, ua)

    @pl.loop(1, CROSS_FIRST)
    def _(j):
        cross_two(j)

    def to_member(d):
        shift = (zs[d // 2 % 2] + cs[d % 2])
        j = lax.rem(y + d // 4, 4) * 4 + shift
        return remote(
            rs.at[rows_of(j)], rb.at[rows_of(mine)], p3_send.at[d], p3_recv, (plane + ys[d // 4] + shift,)
        )

    @pl.when(owner)
    def _():
        seven = pl.ds(0, ZGROUPS - 1)
        pltpu.make_async_copy(tt.at[seven], tt.at[seven], p2_recv).wait()
        qw, kw, vw, gw = [tt[:, i].reshape(128, DH) for i in range(4)]
        s = mm(kw, qw, NT) * SCALE2
        xx = mm(vw, gw, NT)
        top = jnp.max(s, 0, keepdims=True)
        e = jnp.exp2(s - top)
        tot = jnp.sum(e, 0, keepdims=True)
        num = jnp.sum(e * xx, 0, keepdims=True)
        pltpu.make_async_copy(ts.at[seven], ts.at[seven], c2_recv).wait()
        stat = jnp.sum(ts[...], 0)
        near, near_delta, far, far_delta = [stat[i : i + 1] for i in range(4)]
        peak = jnp.maximum(top, jnp.maximum(near, far))
        c_w = jnp.exp2(top - peak)
        c_near = jnp.exp2(near - peak)
        c_far = jnp.exp2(far - peak)
        all_tot = tot * c_w + (c_near + c_far)
        lse = peak + jnp.log2(all_tot)
        delta = (num * c_w + (near_delta * c_near + far_delta * c_far)) / all_tot
        p = e * (c_w / all_tot)
        ds = ((p * FACTOR) * (xx - delta)).astype(BF16)
        wd[0] = mm(ds, kw, TN)
        wd[1] = mm(ds, qw, NN)
        wd[2] = mm(p.astype(BF16), gw, NN)
        own = pl.ds(pl.multiple_of(zg * GROUP, GROUP), GROUP)
        for i in range(3):
            rs[pl.ds(i, GROUP, stride=8), :] = wd[i, own, :]
        rs[pl.ds(3, GROUP, stride=8), :] = jnp.broadcast_to(lse, (GROUP, DH))
        rs[pl.ds(4, GROUP, stride=8), :] = jnp.broadcast_to(delta, (GROUP, DH))

        for d in (10, 11, 9, 8, 6, 7, 14, 15, 4, 5, 12, 13, 2, 3, 1):
            to_member(d).start()

        pltpu.make_async_copy(rs.at[rows_of(m)], rb.at[rows_of(mine)], p3_recv).start()

    @pl.loop(CROSS_FIRST, PAIRS)
    def _(j):
        cross_two(j)

    cross_gather(HEADS - 1, eb)

    wx[0] = jnp.where(row_in_pair[:, :HALF], mm(qr[0], pr[1], NT) * SCALE2, LOW)
    wx[1] = mm(qr[3], pr[2], NT)

    for copy in pair_copies + wide_copies:
        copy.wait_send()
    stat_copy.wait_send()
    wait_sent(sb, pb, p1_send, p1_recv)
    wait_sent(sc, pc, c1_send, c1_recv)

    @pl.when(owner)
    def _():
        for d in range(1, ZGROUPS):
            to_zpeer(tt, p2_send, p2_recv, d).wait_send()
            to_zpeer(ts, c2_send, c2_recv, d).wait_send()

        for d in range(1, GROUP):
            to_member(d).wait_send()

    got = pl.ds(0, 8 * HEADS)
    pltpu.make_async_copy(rb.at[got], rb.at[got], p3_recv).wait()

    all_lse = rb[pl.ds(3, 16, stride=8), :]
    all_delta = rb[pl.ds(4, 16, stride=8), :]
    def at(mask, value):
        return jnp.sum(jnp.where(mask, value, 0.0), 1, keepdims=True)

    lse_r, delta_r = at(here, all_lse), at(here, all_delta)
    lse_f, delta_f = at(other, all_lse), at(other, all_delta)
    p_own = jnp.exp2(ws[0] - lse_r) * weight_wide
    d_own = ((p_own * FACTOR) * (ws[1] - delta_r)).astype(BF16)
    p_cross = jnp.exp2(wx[0] - lse_r)
    d_cross = ((p_cross * FACTOR) * (wx[1] - delta_r)).astype(BF16)
    p_far = jnp.exp2(w2[0] - lse_f)
    d_far = ((p_far * FACTOR) * (w2[1] - delta_f)).astype(BF16)

    def spread(i):
        row = rb[pl.ds(i, 16, stride=8), :]
        return jnp.where(block, jnp.concatenate([row] * HEADS, axis=1), 0.0)

    dq_row = jnp.where(block, mm(d_own, x[1], NN) + mm(d_cross, pr[1], NN), 0.0) + spread(0)
    sel = sel_wide
    blank_left = jnp.zeros((32, TOK), BF16)
    blank_right = jnp.zeros((32, WIDTH), BF16)
    left[0] = jnp.concatenate([sel, sel, blank_left], 0)
    fix[0] = jnp.concatenate([*split(dq_row), blank_right], 0)
    left[1] = jnp.concatenate([d_own, d_far, sel, sel], 0)
    fix[1] = jnp.concatenate([qr[0], qp[0], *split(spread(1))], 0)
    left[2] = jnp.concatenate([p_own.astype(BF16), p_far.astype(BF16), sel, sel], 0)
    fix[2] = jnp.concatenate([qr[3], qp[1], *split(spread(2))], 0)


def finish(acc, left, fix, oq, ok, ov, held, sem):
    stores = []
    for i, ref in enumerate((oq, ok, ov)):
        for part in range(2):
            rows = pl.ds(part * HALF, HALF)
            held[i, rows, :] = (acc[i, rows, :] + mm(left[i, :, rows], fix[i], TN)).astype(BF16)
            stores.append(pltpu.make_async_copy(held.at[i, rows], ref.at[rows], sem.at[2 * i + part]))
            stores[-1].start()
    for store in stores:
        store.wait()


def on_device(query, key, value, grad_out, offsets):
    shape = jax.ShapeDtypeStruct((TOK, WIDTH), BF16)
    vmem = pltpu.VMEM
    dma = pltpu.SemaphoreType.DMA
    acc, left, fix = pl.pallas_call(
        kernel,
        out_shape=(
            jax.ShapeDtypeStruct((3, TOK, WIDTH), F32),
            jax.ShapeDtypeStruct((3, 64, TOK), BF16),
            jax.ShapeDtypeStruct((3, 64, WIDTH), BF16),
        ),
        in_specs=[pl.BlockSpec(memory_space=pltpu.MemorySpace.HBM)] * 5,
        out_specs=(pl.BlockSpec(memory_space=vmem),) * 3,
        scratch_shapes=[
            vmem((4, TOK, WIDTH), BF16),
            vmem((4, HALF, WIDTH), BF16),
            vmem((4, HALF, WIDTH), BF16),
            vmem((4, 16, WIDTH), BF16),
            vmem((8 * HEADS, DH), F32),
            vmem((8 * GROUP, DH), F32),
            vmem((8 * HEADS, DH), F32),
            vmem((8 * GROUP, DH), F32),
            vmem((ZGROUPS, 4, GROUP, DH), BF16),
            vmem((ZGROUPS, 4, DH), F32),
            vmem((8 * GROUP, DH), F32),
            vmem((8 * 16, DH), F32),
            vmem((2, 16, HALF), F32),
            vmem((2, 16, HALF), F32),
            vmem((2, 16, TOK), F32),
            vmem((2, 16, TOK), F32),
            vmem((2, 16, HALF), F32),
            vmem((2, 16, TOK), F32),
            vmem((2, 16, WIDTH), BF16),
            vmem((3, 128, DH), F32),
            pltpu.SMEM((2, HEADS), jnp.int32),
            vmem((2, TOK + HALF, TOK), F32),
            vmem((2, TOK + HALF, TOK), F32),
            vmem((1, TOK), F32),
            vmem((1, TOK), F32),
            vmem((2 * TOK + HALF, TOK), BF16),
            vmem((2 * TOK + HALF, TOK), BF16),
            vmem((2, TOK, HALF), F32),
            vmem((2, TOK, HALF), F32),
            vmem((2, TOK, HALF), BF16),
            vmem((2, TOK, HALF), BF16),
            dma((4,)),
            dma(()),
            pltpu.SemaphoreType.REGULAR((2,)),
            dma((4,)),
            dma((4,)),
            dma((HEADS,)),
            dma(()),
            dma((HEADS,)),
            dma(()),
            dma((ZGROUPS,)),
            dma(()),
            dma((ZGROUPS,)),
            dma(()),
            dma((GROUP,)),
            dma(()),
            dma(()),
            dma(()),
            dma((2,)),
            dma((2,)),
        ],
        compiler_params=pltpu.CompilerParams(collective_id=0, has_side_effects=True, vmem_limit_bytes=48 * 1024 * 1024),
    )(*[pltpu.with_memory_space_constraint(a, pltpu.MemorySpace.HBM) for a in (offsets, query, key, value, grad_out)])
    return pl.pallas_call(
        finish,
        out_shape=(shape, shape, shape),
        in_specs=[pl.BlockSpec(memory_space=vmem)] * 3,
        out_specs=(pl.BlockSpec(memory_space=pl.ANY),) * 3,
        scratch_shapes=[vmem((3, TOK, WIDTH), BF16), dma((6,))],
        compiler_params=pltpu.CompilerParams(vmem_limit_bytes=8 * 1024 * 1024),
    )(acc, left, fix)


def solution(mesh):
    placed = (P("ctx", None),) * 4 + (P(),)
    return jax.shard_map(
        on_device, mesh=mesh, in_specs=placed, out_specs=(P("ctx", None),) * 3, check_vma=False
    )
```

```python
import jax
import jax.numpy as jnp
from jax import lax
from jax.experimental import pallas as pl
from jax.experimental.pallas import tpu as pltpu
from jax.sharding import PartitionSpec as P

MESH = pl.DeviceIdType.MESH
HEADS = 10
DH = 128
TOK = 256
HALF = TOK // 2
WIDTH = HEADS * DH
GROUP = 16
ZGROUPS = 8
FACTOR = DH**-0.5
SCALE2 = FACTOR * 1.4426950408889634
LOW = -1e30
PAIRS = HEADS // 2
CROSS_FIRST = 3
F32 = jnp.float32
BF16 = jnp.bfloat16

NN = (((1,), (0,)), ((), ()))
NT = (((1,), (1,)), ((), ()))
TN = (((0,), (0,)), ((), ()))


def mm(a, b, dims):
    return lax.dot_general(a, b, dims, preferred_element_type=F32)


def iota(shape, dim):
    return lax.broadcasted_iota(jnp.int32, shape, dim)


def split(x):
    high = x.astype(BF16)
    return high, (x - high.astype(F32)).astype(BF16)


def kernel(
    off_hbm, q_hbm, k_hbm, v_hbm, g_hbm, acc, left, fix,
    x, px, pr, qr, sb, pb, sc, pc, tt, ts, rs, rb, lx, lr, ls, ws, wx, w2, qp, wd, off, sa, sb2, ta, tb, da, db, ua, ub, ea, eb,
    ld_sem, off_sem, ready, px_send, px_recv, p1_send, p1_recv, c1_send, c1_recv,
    p2_send, p2_recv, c2_send, c2_recv, p3_send, p3_recv, lx_send, lx_recv, qp_send, qp_recv,
):
    me = lax.axis_index("ctx")
    core = lax.rem(me, 2)
    z = lax.rem(lax.div(me, 2), 16)
    y = lax.rem(lax.div(me, 32), 4)
    base = lax.div(me, 128) * 128
    zg = lax.div(z, 2)
    zl = lax.rem(z, 2)
    m = y * 4 + zl * 2 + core
    turned = lax.rem(zl + lax.div(zg, 4), 2)
    drift = core * (1 - turned)
    mine = (core * 2 + turned) * 4 + lax.rem(y + 2 * lax.rem(zg, 2) * drift, 4)
    owner = mine < HEADS

    def member(j):
        return (base + lax.div(j, 4) * 32 + (zg * 2 + lax.rem(lax.div(j, 2), 2)) * 2 + lax.rem(j, 2),)

    def zpeer(d):
        g = lax.rem(zg + d, ZGROUPS)
        row = lax.rem(y + 2 * (d % 2) * drift, 4)
        return (base + row * 32 + (g * 2 + lax.rem(turned + lax.div(g, 4), 2)) * 2 + core,)

    def owner_of(h):
        k = lax.div(h, 4)
        row = lax.rem(lax.rem(h, 4) + 2 * lax.rem(zg, 2) * lax.div(k, 2), 4)
        return row * 4 + lax.rem(lax.rem(k, 2) + lax.div(zg, 4), 2) * 2 + lax.div(k, 2)

    partner = (me + 1 - 2 * core,)

    def remote(src, dst, send, recv, device):
        return pltpu.make_async_remote_copy(
            src_ref=src, dst_ref=dst, send_sem=send, recv_sem=recv, device_id=device, device_id_type=MESH
        )

    off_load = pltpu.make_async_copy(off_hbm, off, off_sem)
    off_load.start()
    loads = [
        pltpu.make_async_copy(ref, x.at[i], ld_sem.at[i]) for i, ref in enumerate((q_hbm, k_hbm, v_hbm, g_hbm))
    ]
    for i in (1, 2, 0, 3):
        loads[i].start()

    barrier = pltpu.get_barrier_semaphore()
    upper = zpeer(1)
    lower = zpeer(ZGROUPS - 1)
    upper2 = zpeer(2)
    lower2 = zpeer(ZGROUPS - 2)
    for there in (upper2, lower2, upper, lower):
        pl.semaphore_signal(barrier, inc=1, device_id=there, device_id_type=MESH)

    plane = base + zg * 4
    ys = [lax.rem(y + i, 4) * 32 for i in range(4)]
    zs = [zl * 2, 2 - zl * 2]
    cs = [core, 1 - core]
    for i in range(1, GROUP):
        there = plane + ys[i // 4] + (zs[i // 2 % 2] + cs[i % 2])
        pl.semaphore_signal(barrier, inc=1, device_id=(there,), device_id_type=MESH)

    def near_groups_ready():
        @pl.when(owner)
        def _():
            pl.semaphore_signal(ready.at[0], inc=1, device_id=upper2, device_id_type=MESH)
            pl.semaphore_signal(ready.at[1], inc=1, device_id=lower2, device_id_type=MESH)

    sb[...] = jnp.zeros_like(sb)
    sc[...] = jnp.zeros_like(sc)
    rb[...] = jnp.zeros_like(rb)
    rs[...] = jnp.zeros_like(rs)
    ls[...] = jnp.zeros_like(ls)
    perm_row = iota((TOK, TOK), 0)
    perm_to = jnp.where(perm_row < HALF, 2 * perm_row, 2 * perm_row - (TOK - 1))
    perm = (iota((TOK, TOK), 1) == perm_to).astype(F32).astype(BF16)
    block = lax.div(iota((16, WIDTH), 1), DH) == iota((16, WIDTH), 0)
    lane_head = lax.div(iota((8, WIDTH), 1), DH)
    row16 = iota((16, TOK), 0)
    lane16 = iota((16, TOK), 1)

    off_load.wait()
    off_lane = jnp.zeros((8, WIDTH), jnp.int32)
    off0 = jnp.zeros((16, TOK), jnp.int32)
    off1 = jnp.zeros((16, TOK), jnp.int32)
    for h in range(HEADS):
        off_lane = jnp.where(lane_head == h, off[0, h], off_lane)
        off0 = jnp.where(row16 == h, off[0, h], off0)
        off1 = jnp.where(row16 == h, off[1, h], off1)
    sel_wide = (lane16 == off1).astype(F32).astype(BF16)
    row_in_pair = lax.rem(off1, 2) == off0
    key_in_pair = lax.rem(lane16, 2) == off0
    both = jnp.logical_and(row_in_pair, key_in_pair)
    weight_wide = jnp.where(both, 2.0, 1.0)
    off_wide = off_lane[0:1, :] > 0

    def pack_pair(i):
        parts = mm(perm, x[i], NN)
        px[i] = jnp.where(off_wide, parts[HALF:], parts[:HALF]).astype(BF16)

    pair_copies = [remote(px.at[i], pr.at[i], px_send.at[i], px_recv.at[i], partner) for i in range(4)]

    def rows_of(j):
        return pl.ds(pl.multiple_of(8 * j, 8), 8)

    def to_owner(src, dst, send, recv, h):
        return remote(src.at[rows_of(h)], dst.at[rows_of(m)], send.at[h], recv, member(owner_of(h)))

    def send_to_owners(src, dst, send, recv):
        @pl.loop(0, HEADS)
        def _(h):
            @pl.when(owner_of(h) != m)
            def _():
                to_owner(src, dst, send, recv, h).start()

        @pl.when(owner)
        def _():
            pltpu.make_async_copy(src.at[rows_of(mine)], dst.at[rows_of(m)], recv).start()

    def wait_sent(src, dst, send, recv):
        @pl.loop(0, HEADS)
        def _(h):
            @pl.when(owner_of(h) != m)
            def _():
                to_owner(src, dst, send, recv, h).wait_send()

    loads[1].wait()
    pack_pair(1)
    loads[2].wait()
    pack_pair(2)
    loads[0].wait()
    loads[3].wait()
    for i in range(4):
        picked = jnp.where(block, mm(sel_wide, x[i], NN), 0.0)
        qr[i] = picked.astype(BF16)
        for h in range(HEADS):
            sb[8 * h + i : 8 * h + i + 1, :] = picked[h : h + 1, h * DH : (h + 1) * DH]

    s_own = mm(qr[0], x[1], NT) * SCALE2
    x_own = mm(qr[3], x[2], NT)
    ws[0] = s_own
    ws[1] = x_own
    lane128 = iota((16, DH), 1)
    token = zg * GROUP + m
    here = lane128 == token
    other = lane128 == token + 1 - 2 * core

    def statistics(s, value, weight, row, at):
        peak = jnp.max(s, 1, keepdims=True)
        e = jnp.exp2(s - peak)
        e = e if weight is None else e * weight
        total = jnp.sum(e, 1, keepdims=True)
        blend = jnp.sum(e * value, 1, keepdims=True)
        lse = jnp.where(at, peak + jnp.log2(total), 0.0)
        delta = jnp.where(at, blend / total, 0.0)
        for h in range(HEADS):
            sc[8 * h + row : 8 * h + row + 1, :] = lse[h : h + 1, :]
            sc[8 * h + row + 1 : 8 * h + row + 2, :] = delta[h : h + 1, :]

    statistics(s_own, x_own, weight_wide, 0, here)

    pl.semaphore_wait(barrier, GROUP + 3)
    near_groups_ready()
    wide_copies = [remote(qr.at[3 * i], qp.at[i], qp_send.at[i], qp_recv.at[i], partner) for i in range(2)]
    for copy in wide_copies:
        copy.start()
    send_to_owners(sb, pb, p1_send, p1_recv)
    pair_copies[1].start()
    pair_copies[2].start()

    for copy in wide_copies:
        copy.wait_recv()
    s_far = jnp.where(row_in_pair[:, :HALF], mm(qp[0], px[1], NT) * SCALE2, LOW)
    statistics(s_far, mm(qp[1], px[2], NT), None, 2, other)
    send_to_owners(sc, pc, c1_send, c1_recv)

    pack_pair(0)
    pair_copies[0].start()
    pack_pair(3)
    pair_copies[3].start()

    lane_row = iota((1, TOK), 1)
    parity_lane = lax.rem(lane_row, 2)
    parity_sub = lax.rem(iota((1, 8, TOK), 1), 2)
    parity_both = lax.rem(iota((1, 8, TOK), 2), 2)

    def total_of(a):
        return jnp.sum(jnp.sum(a, 0), 0, keepdims=True)

    def peak_of(a):
        return jnp.max(jnp.max(a, 0), 0, keepdims=True)

    def lanes(h):
        return pl.ds(pl.multiple_of(h * DH, DH), DH)

    def products(h, sx, top_ref):
        hs = lanes(h)
        qh = x[0, :, hs]
        gh = x[3, :, hs]
        s0 = mm(x[1, :, hs], qh, NT) * SCALE2
        s1 = mm(pr[1, :, hs], qh, NT) * SCALE2 + jnp.where(parity_lane == off[0, h], 0.0, LOW)
        sx[0, :TOK, :] = s0
        sx[0, TOK:, :] = s1
        sx[1, :TOK, :] = mm(x[2, :, hs], gh, NT)
        sx[1, TOK:, :] = mm(pr[2, :, hs], gh, NT)
        top = jnp.maximum(peak_of(s0.reshape(TOK // 8, 8, TOK)), peak_of(s1.reshape(HALF // 8, 8, TOK)))
        top_ref[...] = top

    def weigh(h, sx, top_ref, pd):
        top = top_ref[...]
        keep = jnp.where(lane_row == off[1, h], 0.0, 1.0)
        twice = jnp.logical_and(parity_sub == off[0, h], parity_both == off[0, h])
        lifted = top[None] - jnp.where(twice, 1.0, 0.0)
        e0 = jnp.exp2(sx[0, :TOK, :].reshape(TOK // 8, 8, TOK) - lifted)
        e1 = jnp.exp2(sx[0, TOK:, :].reshape(HALF // 8, 8, TOK) - top)
        x0 = sx[1, :TOK, :].reshape(TOK // 8, 8, TOK)
        x1 = sx[1, TOK:, :].reshape(HALF // 8, 8, TOK)
        tot = total_of(e0) + total_of(e1)
        num = total_of(e0 * x0) + total_of(e1 * x1)
        inv = 1.0 / tot
        delta = num * inv
        ls[0, pl.ds(h, 1), :] = jnp.where(keep > 0, top + jnp.log2(tot), -LOW)
        ls[1, pl.ds(h, 1), :] = delta
        gain = inv * keep
        slope = gain * FACTOR
        pd[:TOK, :] = (e0 * gain).reshape(TOK, TOK).astype(BF16)
        pd[TOK : 2 * TOK, :] = ((e0 * slope) * (x0 - delta)).reshape(TOK, TOK).astype(BF16)
        pd[2 * TOK :, :] = ((e1 * slope) * (x1 - delta)).reshape(HALF, TOK).astype(BF16)

    def gather(h, pd):
        hs = lanes(h)
        acc[2, :, hs] = mm(pd[:TOK, :], x[3, :, hs], NN)
        acc[1, :, hs] = mm(pd[TOK : 2 * TOK, :], x[0, :, hs], NN)
        acc[0, :, hs] = mm(pd[TOK : 2 * TOK, :], x[1, :, hs], TN) + mm(pd[2 * TOK :, :], pr[1, :, hs], TN)

    def to_zpeer(src, send, recv, d):
        return remote(src.at[zg], src.at[zg], send.at[d], recv, zpeer(d))

    @pl.when(owner)
    def _():
        pltpu.make_async_copy(pb, pb, p1_recv).wait()
        for i in range(4):
            tt[zg, i] = pb[pl.ds(i, GROUP, stride=8), :].astype(BF16)
        for d in (2, 6):
            to_zpeer(tt, p2_send, p2_recv, d).start()
        pl.semaphore_wait(ready.at[0], 1)
        pl.semaphore_wait(ready.at[1], 1)
        for d in (4, 3, 5):
            to_zpeer(tt, p2_send, p2_recv, d).start()

    pair_copies[1].wait_recv()
    pair_copies[2].wait_recv()
    products(0, sa, ta)
    weigh(0, sa, ta, da)
    products(1, sb2, tb)
    gather(0, da)
    weigh(1, sb2, tb, db)
    products(2, sa, ta)

    @pl.when(owner)
    def _():
        pltpu.make_async_copy(pc, pc, c1_recv).wait()
        for i in range(4):
            ts[zg, i : i + 1, :] = jnp.sum(pc[pl.ds(i, GROUP, stride=8), :], 0, keepdims=True)
        for d in (4, 3, 5, 2, 6, 1, 7):
            to_zpeer(ts, c2_send, c2_recv, d).start()
        for d in (1, 7):
            to_zpeer(tt, p2_send, p2_recv, d).start()

    @pl.loop(1, PAIRS)
    def _(j):
        gather(2 * j - 1, db)
        weigh(2 * j, sa, ta, da)
        products(2 * j + 1, sb2, tb)
        gather(2 * j, da)
        weigh(2 * j + 1, sb2, tb, db)
        products(jnp.minimum(2 * j + 2, HEADS - 1), sa, ta)

    gather(HEADS - 1, db)

    perm_t = jnp.where(iota((TOK, TOK), 1) < HALF, 2 * iota((TOK, TOK), 1), 2 * iota((TOK, TOK), 1) - (TOK - 1))
    perm_t = (iota((TOK, TOK), 0) == perm_t).astype(F32).astype(BF16)
    for i in range(2):
        value = ls[i]
        high, rest = split(value)
        mid, least = split(value - high.astype(F32))
        moved = mm(high, perm_t, NN) + (mm(mid, perm_t, NN) + mm(least, perm_t, NN))
        lx[i] = jnp.where(off0[:, :HALF] > 0, moved[:, HALF:], moved[:, :HALF])
    stat_copy = remote(lx, lr, lx_send, lx_recv, partner)
    stat_copy.start()

    pair_copies[0].wait_recv()
    pair_copies[3].wait_recv()
    stat_copy.wait_recv()

    def cross_products(h, sx):
        hs = lanes(h)
        sx[0] = mm(x[1, :, hs], pr[0, :, hs], NT) * SCALE2
        sx[1] = mm(x[2, :, hs], pr[3, :, hs], NT)

    def cross_weigh(h, sx, pd):
        lse = lr[0, pl.ds(h, 1), :]
        delta = lr[1, pl.ds(h, 1), :]
        s2 = sx[0].reshape(TOK // 8, 8, HALF)
        x2 = sx[1].reshape(TOK // 8, 8, HALF)
        p2 = jnp.exp2(jnp.where(parity_sub[:, :, :HALF] == off[0, h], s2 - lse, LOW))
        pd[0] = p2.reshape(TOK, HALF).astype(BF16)
        pd[1] = ((p2 * FACTOR) * (x2 - delta)).reshape(TOK, HALF).astype(BF16)

    def cross_gather(h, pd):
        hs = lanes(h)
        acc[2, :, hs] += mm(pd[0], pr[3, :, hs], NN)
        acc[1, :, hs] += mm(pd[1], pr[0, :, hs], NN)

    def cross_two(j):
        cross_gather(2 * j - 1, eb)
        cross_weigh(2 * j, ua, ea)
        cross_products(2 * j + 1, ub)
        cross_gather(2 * j, ea)
        cross_weigh(2 * j + 1, ub, eb)
        cross_products(jnp.minimum(2 * j + 2, HEADS - 1), ua)

    cross_products(0, ua)
    cross_weigh(0, ua, ea)
    cross_products(1, ub)
    cross_gather(0, ea)
    cross_weigh(1, ub, eb)
    cross_products(2, ua)

    @pl.loop(1, CROSS_FIRST)
    def _(j):
        cross_two(j)

    wx[0] = jnp.where(row_in_pair[:, :HALF], mm(qr[0], pr[1], NT) * SCALE2, LOW)
    wx[1] = mm(qr[3], pr[2], NT)
    w2[0] = jnp.where(both, mm(qp[0], x[1], NT) * SCALE2, LOW)
    w2[1] = mm(qp[1], x[2], NT)

    def to_member(d):
        shift = (zs[d // 2 % 2] + cs[d % 2])
        j = lax.rem(y + d // 4, 4) * 4 + shift
        return remote(
            rs.at[rows_of(j)], rb.at[rows_of(mine)], p3_send.at[d], p3_recv, (plane + ys[d // 4] + shift,)
        )

    @pl.when(owner)
    def _():
        seven = pl.ds(0, ZGROUPS - 1)
        pltpu.make_async_copy(tt.at[seven], tt.at[seven], p2_recv).wait()
        qw, kw, vw, gw = [tt[:, i].reshape(128, DH) for i in range(4)]
        s = mm(kw, qw, NT) * SCALE2
        xx = mm(vw, gw, NT)
        top = jnp.max(s, 0, keepdims=True)
        e = jnp.exp2(s - top)
        tot = jnp.sum(e, 0, keepdims=True)
        num = jnp.sum(e * xx, 0, keepdims=True)
        pltpu.make_async_copy(ts.at[seven], ts.at[seven], c2_recv).wait()
        stat = jnp.sum(ts[...], 0)
        near, near_delta, far, far_delta = [stat[i : i + 1] for i in range(4)]
        peak = jnp.maximum(top, jnp.maximum(near, far))
        c_w = jnp.exp2(top - peak)
        c_near = jnp.exp2(near - peak)
        c_far = jnp.exp2(far - peak)
        all_tot = tot * c_w + (c_near + c_far)
        lse = peak + jnp.log2(all_tot)
        delta = (num * c_w + (near_delta * c_near + far_delta * c_far)) / all_tot
        p = e * (c_w / all_tot)
        ds = ((p * FACTOR) * (xx - delta)).astype(BF16)
        wd[0] = mm(ds, kw, TN)
        wd[1] = mm(ds, qw, NN)
        wd[2] = mm(p.astype(BF16), gw, NN)
        own = pl.ds(pl.multiple_of(zg * GROUP, GROUP), GROUP)
        for i in range(3):
            rs[pl.ds(i, GROUP, stride=8), :] = wd[i, own, :]
        rs[pl.ds(3, GROUP, stride=8), :] = jnp.broadcast_to(lse, (GROUP, DH))
        rs[pl.ds(4, GROUP, stride=8), :] = jnp.broadcast_to(delta, (GROUP, DH))

        for d in (10, 11, 9, 8, 6, 7, 14, 15, 4, 5, 12, 13, 2, 3, 1):
            to_member(d).start()

        pltpu.make_async_copy(rs.at[rows_of(m)], rb.at[rows_of(mine)], p3_recv).start()

    @pl.loop(CROSS_FIRST, PAIRS)
    def _(j):
        cross_two(j)

    cross_gather(HEADS - 1, eb)

    for copy in pair_copies + wide_copies:
        copy.wait_send()
    stat_copy.wait_send()
    wait_sent(sb, pb, p1_send, p1_recv)
    wait_sent(sc, pc, c1_send, c1_recv)

    @pl.when(owner)
    def _():
        for d in range(1, ZGROUPS):
            to_zpeer(tt, p2_send, p2_recv, d).wait_send()
            to_zpeer(ts, c2_send, c2_recv, d).wait_send()

        for d in range(1, GROUP):
            to_member(d).wait_send()

    got = pl.ds(0, 8 * HEADS)
    pltpu.make_async_copy(rb.at[got], rb.at[got], p3_recv).wait()

    all_lse = rb[pl.ds(3, 16, stride=8), :]
    all_delta = rb[pl.ds(4, 16, stride=8), :]
    def at(mask, value):
        return jnp.sum(jnp.where(mask, value, 0.0), 1, keepdims=True)

    lse_r, delta_r = at(here, all_lse), at(here, all_delta)
    lse_f, delta_f = at(other, all_lse), at(other, all_delta)
    p_own = jnp.exp2(ws[0] - lse_r) * weight_wide
    d_own = ((p_own * FACTOR) * (ws[1] - delta_r)).astype(BF16)
    p_cross = jnp.exp2(wx[0] - lse_r)
    d_cross = ((p_cross * FACTOR) * (wx[1] - delta_r)).astype(BF16)
    p_far = jnp.exp2(w2[0] - lse_f)
    d_far = ((p_far * FACTOR) * (w2[1] - delta_f)).astype(BF16)

    def spread(i):
        row = rb[pl.ds(i, 16, stride=8), :]
        return jnp.where(block, jnp.concatenate([row] * HEADS, axis=1), 0.0)

    dq_row = jnp.where(block, mm(d_own, x[1], NN) + mm(d_cross, pr[1], NN), 0.0) + spread(0)
    sel = sel_wide
    blank_left = jnp.zeros((32, TOK), BF16)
    blank_right = jnp.zeros((32, WIDTH), BF16)
    left[0] = jnp.concatenate([sel, sel, blank_left], 0)
    fix[0] = jnp.concatenate([*split(dq_row), blank_right], 0)
    left[1] = jnp.concatenate([d_own, d_far, sel, sel], 0)
    fix[1] = jnp.concatenate([qr[0], qp[0], *split(spread(1))], 0)
    left[2] = jnp.concatenate([p_own.astype(BF16), p_far.astype(BF16), sel, sel], 0)
    fix[2] = jnp.concatenate([qr[3], qp[1], *split(spread(2))], 0)


def finish(acc, left, fix, oq, ok, ov, held, sem):
    stores = []
    for i, ref in enumerate((oq, ok, ov)):
        for part in range(2):
            rows = pl.ds(part * HALF, HALF)
            held[i, rows, :] = (acc[i, rows, :] + mm(left[i, :, rows], fix[i], TN)).astype(BF16)
            stores.append(pltpu.make_async_copy(held.at[i, rows], ref.at[rows], sem.at[2 * i + part]))
            stores[-1].start()
    for store in stores:
        store.wait()


def on_device(query, key, value, grad_out, offsets):
    shape = jax.ShapeDtypeStruct((TOK, WIDTH), BF16)
    vmem = pltpu.VMEM
    dma = pltpu.SemaphoreType.DMA
    acc, left, fix = pl.pallas_call(
        kernel,
        out_shape=(
            jax.ShapeDtypeStruct((3, TOK, WIDTH), F32),
            jax.ShapeDtypeStruct((3, 64, TOK), BF16),
            jax.ShapeDtypeStruct((3, 64, WIDTH), BF16),
        ),
        in_specs=[pl.BlockSpec(memory_space=pltpu.MemorySpace.HBM)] * 5,
        out_specs=(pl.BlockSpec(memory_space=vmem),) * 3,
        scratch_shapes=[
            vmem((4, TOK, WIDTH), BF16),
            vmem((4, HALF, WIDTH), BF16),
            vmem((4, HALF, WIDTH), BF16),
            vmem((4, 16, WIDTH), BF16),
            vmem((8 * HEADS, DH), F32),
            vmem((8 * GROUP, DH), F32),
            vmem((8 * HEADS, DH), F32),
            vmem((8 * GROUP, DH), F32),
            vmem((ZGROUPS, 4, GROUP, DH), BF16),
            vmem((ZGROUPS, 4, DH), F32),
            vmem((8 * GROUP, DH), F32),
            vmem((8 * 16, DH), F32),
            vmem((2, 16, HALF), F32),
            vmem((2, 16, HALF), F32),
            vmem((2, 16, TOK), F32),
            vmem((2, 16, TOK), F32),
            vmem((2, 16, HALF), F32),
            vmem((2, 16, TOK), F32),
            vmem((2, 16, WIDTH), BF16),
            vmem((3, 128, DH), F32),
            pltpu.SMEM((2, HEADS), jnp.int32),
            vmem((2, TOK + HALF, TOK), F32),
            vmem((2, TOK + HALF, TOK), F32),
            vmem((1, TOK), F32),
            vmem((1, TOK), F32),
            vmem((2 * TOK + HALF, TOK), BF16),
            vmem((2 * TOK + HALF, TOK), BF16),
            vmem((2, TOK, HALF), F32),
            vmem((2, TOK, HALF), F32),
            vmem((2, TOK, HALF), BF16),
            vmem((2, TOK, HALF), BF16),
            dma((4,)),
            dma(()),
            pltpu.SemaphoreType.REGULAR((2,)),
            dma((4,)),
            dma((4,)),
            dma((HEADS,)),
            dma(()),
            dma((HEADS,)),
            dma(()),
            dma((ZGROUPS,)),
            dma(()),
            dma((ZGROUPS,)),
            dma(()),
            dma((GROUP,)),
            dma(()),
            dma(()),
            dma(()),
            dma((2,)),
            dma((2,)),
        ],
        compiler_params=pltpu.CompilerParams(collective_id=0, has_side_effects=True, vmem_limit_bytes=48 * 1024 * 1024),
    )(*[pltpu.with_memory_space_constraint(a, pltpu.MemorySpace.HBM) for a in (offsets, query, key, value, grad_out)])
    return pl.pallas_call(
        finish,
        out_shape=(shape, shape, shape),
        in_specs=[pl.BlockSpec(memory_space=vmem)] * 3,
        out_specs=(pl.BlockSpec(memory_space=pl.ANY),) * 3,
        scratch_shapes=[vmem((3, TOK, WIDTH), BF16), dma((6,))],
        compiler_params=pltpu.CompilerParams(vmem_limit_bytes=8 * 1024 * 1024),
    )(acc, left, fix)


def solution(mesh):
    placed = (P("ctx", None),) * 4 + (P(),)
    return jax.shard_map(
        on_device, mesh=mesh, in_specs=placed, out_specs=(P("ctx", None),) * 3, check_vma=False
    )
```
